32 devices in a mesh: gz: 8 (over z, y), xy: 4 (over x, core).
Axes of the slice: x: 2, y: 2, z: 4, core: 2. Of those that a mesh axis runs over, the one named last changes fastest.
Arguments:
- up_source: bfloat16 [8, 2, 32, 1024], P('gz', None, None, 'xy'), may hold values from -6 to 6
- down_source: bfloat16 [8, 2, 32, 1024], P('gz', None, None, 'xy'), may hold values from -6 to 6
- source_layer: int32 [32], replicated, may hold values from 0 to 7, as said below
- u_factor: bfloat16 [8, 4, 4, 2, 128, 256], P('gz', 'xy'), may hold values from -0.15625 to 0.15625
- v_factor: bfloat16 [8, 4, 4, 2, 128, 256], P('gz', 'xy'), may hold values from -0.25 to 0.25
- block_rank: int32 [8, 4, 4], P('gz', 'xy'), may hold values from 1 to 4
Outputs:
- up_trace: bfloat16 [8, 2, 32, 1024], P('gz', None, None, 'xy')
- down_trace: bfloat16 [8, 2, 32, 1024], P('gz', None, None, 'xy')
The draws below stay inside these ranges and needn't reach their ends.
Inputs may be any that keep to these rules, and one draw needn't show every extreme that they name: `source_layer`: the index of the layer slab in which source s lies; source 0 lies in slab 0 and source 1 in slab 8 - 1. `block_rank`: block (i, j) of interface l has rank 32 times this number.
All inputs are finite; a program needn't handle non-finite values.
Results may differ from the reference program's by a relative error of at most 0.007.
Values may be sent and summed in bfloat16 or wider, within the bound.
A program may use at most 64 MiB of HBM per device.

```python
import jax
import jax.numpy as jnp
from jax import lax

BLK = 256
RMAX = 128
SRC = 32
STEPS = 3
LAYERS = 8
N = 1024
NB = 4
RANK_STEP = 32


def draw_source_layer(key, part):
    drawn = jax.random.randint(key, (SRC,), 0, LAYERS, dtype=jnp.int32)
    position = jnp.arange(SRC, dtype=jnp.int32)
    drawn = jnp.where(position == 0, jnp.zeros_like(drawn), drawn)
    drawn = jnp.where(position == 1, jnp.full_like(drawn, LAYERS - 1), drawn)
    return drawn


def set_ends(result, stream_key, least, largest):
    longest = result.shape.index(max(result.shape))
    spots = []
    for shift in (0, 1):
        where = [jax.random.randint(jax.random.fold_in(stream_key, axis), (), 0, length) for axis, length in enumerate(result.shape)]
        where[longest] = (where[longest] + shift) % result.shape[longest]
        spots.append(tuple(where))
    return result.at[spots[0]].set(least).at[spots[1]].set(largest)


def shard_levels(own_key, shape, split, low, high):
    def one(dim, parts):
        draws = jax.random.uniform(jax.random.fold_in(jax.random.fold_in(own_key, 6), dim), (parts,), jnp.float32, low / len(split), high / len(split))
        return jnp.repeat(jnp.exp(draws), shape[dim] // parts).reshape((-1,) + (1,) * (len(shape) - dim - 1))

    level = one(*split[0])
    for cut in split[1:]:
        level = level * one(*cut)
    return level


def bell_draw(rng, dims, spread, most, shards=(), held_as=jnp.bfloat16):
    level = shard_levels(rng, dims, shards, -0.22, 0.18) if shards else 1.0
    entries = jax.random.normal(rng, dims, jnp.float32) * spread * level
    return jnp.minimum(jnp.maximum(entries, -most), most).astype(held_as)


def setup_inputs(seed: int = 0) -> dict:
    key_of = jax.random.split(jax.random.key(seed), 7)
    up_source = bell_draw(key_of[0], (LAYERS, 2, SRC, N), 1.0, 6.0, ((0, 8), (3, 4)))
    down_source = bell_draw(key_of[1], (LAYERS, 2, SRC, N), 1.0, 6.0, ((0, 8), (3, 4)))
    source_layer = draw_source_layer(jax.random.fold_in(key_of[6], 71), 0)
    u_factor = bell_draw(key_of[3], (LAYERS, NB, NB, 2, RMAX, BLK), (3 * NB * RMAX) ** -0.5, 0.15625, ((0, 8), (1, 4)))
    v_factor = bell_draw(key_of[4], (LAYERS, NB, NB, 2, RMAX, BLK), (2 * BLK) ** -0.5, 0.25, ((0, 8), (1, 4)))
    block_rank = set_ends(jax.random.randint(key_of[5], (LAYERS, NB, NB), 1, 5), jax.random.fold_in(key_of[5], 1), 1, 4).astype(jnp.int32)
    return dict(up_source=up_source, down_source=down_source, source_layer=source_layer, u_factor=u_factor, v_factor=v_factor, block_rank=block_rank)


def complex_parts(product):
    real = product[..., 0, :, 0, :] - product[..., 1, :, 1, :]
    imag = product[..., 0, :, 1, :] + product[..., 1, :, 0, :]
    return jnp.stack([real, imag], axis=-3)


def round_half(values):
    return lax.optimization_barrier(values.astype(jnp.bfloat16)).astype(jnp.float32)


def layer_apply(u_layer, v_layer, rank_layer, up_layer, above_layer):
    keep_rank = jnp.arange(RMAX, dtype=jnp.int32)[None, None, :] < RANK_STEP * rank_layer[:, :, None]
    u_float = u_layer.astype(jnp.float32)
    v_float = v_layer.astype(jnp.float32)
    pieces = up_layer.astype(jnp.float32).reshape(2, SRC, NB, BLK)
    up_coef = complex_parts(jnp.einsum('asjb,ijcrb->ijascr', pieces, v_float))
    up_coef = round_half(jnp.where(keep_rank[:, :, None, None, :], up_coef, 0.0))
    forward = complex_parts(jnp.einsum('ijasr,ijcrb->iascb', up_coef, u_float))
    forward = jnp.transpose(forward, (1, 2, 0, 3)).reshape(2, SRC, N)
    upper = above_layer.astype(jnp.float32).reshape(2, SRC, NB, BLK)
    down_coef = complex_parts(jnp.einsum('asib,ijcrb->ijascr', upper, u_float))
    down_coef = round_half(jnp.where(keep_rank[:, :, None, None, :], down_coef, 0.0))
    backward = complex_parts(jnp.einsum('ijasr,ijcrb->jascb', down_coef, v_float))
    backward = jnp.transpose(backward, (1, 2, 0, 3)).reshape(2, SRC, N)
    return forward, backward


def reference(up_source, down_source, source_layer, u_factor, v_factor, block_rank):
    layer_ids = jnp.arange(LAYERS, dtype=jnp.int32)
    up_mask = (layer_ids[:, None] >= source_layer[None, :])[:, None, :, None]
    down_mask = (layer_ids[:, None] <= source_layer[None, :])[:, None, :, None]
    active_up = jnp.where(up_mask, up_source, jnp.zeros_like(up_source))
    active_down = jnp.where(down_mask, down_source, jnp.zeros_like(down_source))
    up_trace = active_up
    down_trace = active_down
    for sweep_index in range(STEPS):
        upper = jnp.concatenate([down_trace[1:], jnp.zeros_like(down_trace[:1])], axis=0)
        forward, backward = lax.map(lambda items: layer_apply(*items), (u_factor, v_factor, block_rank, up_trace, upper))
        lower = jnp.concatenate([jnp.zeros_like(forward[:1]), forward[:-1]], axis=0)
        up_trace = (active_up.astype(jnp.float32) + lower).astype(jnp.bfloat16)
        down_trace = (active_down.astype(jnp.float32) + backward).astype(jnp.bfloat16)
    return up_trace, down_trace
```

```python
import functools

import jax
import jax.numpy as jnp
from jax import lax
from jax.experimental import pallas as pl
from jax.experimental.pallas import tpu as pltpu
from jax.sharding import PartitionSpec as P

STEPS = 3
MESH = pl.DeviceIdType.MESH
F32, BF16 = jnp.float32, jnp.bfloat16


def kernel(
    layers, n, up_hbm, down_hbm, layer_hbm, u_hbm, v_hbm, rank_hbm, up_out, down_out,
    up_ref, down_ref, layer_ref, rank_ref, u_mem, v_mem,
    up_own, down_own, up_all, first_in, forward_mem, backward_mem,
    first_term, twin_term, base, up_in, up_send, down_in, down_send,
    up_last_in, up_last_send, down_last_in, down_last_send,
    small_sem, u_sem, v_sem, gather_ssem, gather_rsem, first_ssem, first_rsem,
    back_ssem, back_rsem, forw_ssem, forw_rsem, term_ssem, term_rsem,
    up_ssem0, up_rsem0, up_ssem, up_rsem, up_last_ssem, up_last_rsem,
    down_ssem, down_rsem, down_last_ssem, down_last_rsem,
):
    layer = lax.axis_index("gz")
    me = lax.axis_index("xy")
    has_above = layer < layers - 1
    has_below = layer > 0
    chips = n // 2
    chip = me // 2
    core = lax.rem(me, 2)
    twin = me + 1 - 2 * core
    _, sources, width = up_ref.shape
    half = sources // 2
    rows = 2 * half
    max_rank = u_mem.shape[2]
    chip_order = [lax.rem(chip + k, chips) for k in range(chips)]
    far_chips = [*chip_order[1:], chip]

    def remote(src, dst, ssem, rsem, to_layer, to_block):
        return pltpu.make_async_remote_copy(
            src_ref=src, dst_ref=dst, send_sem=ssem, recv_sem=rsem,
            device_id={"gz": to_layer, "xy": to_block}, device_id_type=MESH,
        )

    def arrived(ref, rsem):
        remote(ref, ref, term_ssem, rsem, layer, me).wait_recv()

    barrier = pltpu.get_barrier_semaphore()

    def greet(to_layer, to_block):
        pl.semaphore_signal(
            barrier, inc=1, device_id={"gz": to_layer, "xy": to_block}, device_id_type=MESH
        )

    @pl.when(has_below)
    def _():
        for k in range(n):
            greet(layer - 1, k)

    @pl.when(has_above)
    def _():
        for k in range(n):
            greet(layer + 1, k)

    for k in range(1, n):
        greet(layer, lax.rem(me + k, n))

    small = [
        pltpu.make_async_copy(src, dst, small_sem.at[i])
        for i, (src, dst) in enumerate(
            [(layer_hbm, layer_ref), (up_hbm.at[0], up_ref), (down_hbm.at[0], down_ref), (rank_hbm, rank_ref)]
        )
    ]
    for load in small:
        load.start()
    load_u = [pltpu.make_async_copy(u_hbm.at[0, 0, j], u_mem.at[j], u_sem.at[j]) for j in range(n)]
    load_v = [pltpu.make_async_copy(v_hbm.at[0, 0, j], v_mem.at[j], v_sem.at[j]) for j in range(n)]
    for j in range(n):
        load_u[j].start()
        load_v[j].start()
    for load in small:
        load.wait()

    square = (sources, sources)
    diagonal = lax.broadcasted_iota(jnp.int32, square, 0) == lax.broadcasted_iota(jnp.int32, square, 1)
    source_layer = jnp.sum(
        jnp.where(diagonal, jnp.broadcast_to(layer_ref[...], square), 0), axis=1, keepdims=True
    )
    source_layer = jnp.broadcast_to(source_layer, (sources, width))
    for ref, own, keep in (
        (up_ref, up_own, layer >= source_layer), (down_ref, down_own, layer <= source_layer),
    ):
        for part in range(2):
            masked = jnp.where(keep, ref[part].astype(F32), 0.0).astype(BF16)
            for h in range(2):
                own[h, part * half:(part + 1) * half] = masked[h * half:(h + 1) * half]

    @pl.when(jnp.logical_not(has_below))
    def _():
        up_in[...] = jnp.zeros_like(up_in)
        up_last_in[...] = jnp.zeros_like(up_last_in)

    @pl.when(jnp.logical_not(has_above))
    def _():
        first_in[...] = jnp.zeros_like(first_in)
        down_in[...] = jnp.zeros_like(down_in)

    peers = n - 1 + jnp.where(has_above, n, 0) + jnp.where(has_below, n, 0)
    pl.semaphore_wait(barrier, peers)

    def gather(k):
        to = lax.rem(me + k, n)
        return remote(up_own, up_all.at[me], gather_ssem.at[k], gather_rsem.at[me], layer, to)

    def first(h):
        return remote(
            down_own.at[h], first_in.at[core], first_ssem.at[h], first_rsem.at[core], layer - 1, 2 * chip + h
        )

    def give_backward(j):
        slot = backward_mem.at[j, core]
        return remote(slot, slot, back_ssem.at[j], back_rsem.at[j], layer, twin)

    def give_forward(j):
        slot = forward_mem.at[core, j]
        return remote(slot, slot, forw_ssem.at[j], forw_rsem.at[j], layer, twin)

    give_term = remote(twin_term, first_term.at[core], term_ssem, term_rsem, layer, twin)

    def up_step0(q, h):
        return remote(
            up_send.at[0, h], up_in.at[0, me], up_ssem0.at[2 * q + h], up_rsem0.at[me], layer + 1, 2 * q + h
        )

    def up_step1(q):
        return remote(
            up_send.at[1], up_in.at[1, pl.ds(2 * chip, 2)], up_ssem.at[q], up_rsem.at[chip],
            layer + 1, 2 * q + core,
        )

    def up_last(h):
        return remote(
            up_last_send.at[h], up_last_in.at[core], up_last_ssem.at[h], up_last_rsem.at[core],
            layer + 1, 2 * chip + h,
        )

    def down_step(t, q):
        return remote(
            down_send.at[t, pl.ds(2 * q, 2)], down_in.at[t, chip], down_ssem.at[t, q], down_rsem.at[t, chip],
            layer - 1, 2 * q + core,
        )

    def down_last(k):
        to = lax.rem(me + k, n)
        return remote(
            down_last_send.at[to], down_last_in.at[me], down_last_ssem.at[k], down_last_rsem.at[me], layer, to
        )

    far_first = [*range(2, n), 1]

    @pl.when(has_below)
    def _():
        for h in range(2):
            first(h).start()

    for k in far_first:
        gather(k).start()

    rank_index = lax.rem(lax.broadcasted_iota(jnp.int32, (2 * max_rank, width), 0), max_rank)

    def factors(j):
        keep = rank_index < (max_rank // 4) * rank_ref[0, 0, j]
        u = u_mem[j].reshape(2 * max_rank, width)
        return jnp.where(keep, u, jnp.zeros_like(u)), v_mem[j].reshape(2 * max_rank, width)

    def paired(x):
        return jnp.concatenate([x[:max_rank], -x[max_rank:]], axis=0), jnp.concatenate(
            [x[max_rank:], x[:max_rank]], axis=0
        )

    def outer(a, b):
        return lax.dot_general(a, b, (((0,), (0,)), ((), ())), preferred_element_type=F32).astype(BF16)

    for j in range(n):
        load_u[j].wait()
        load_v[j].wait()
        u, v = factors(j)
        for part, right in enumerate(paired(v)):
            backward_mem[j, core, part] = outer(u, right)
        give_backward(j).start()
    for j in range(n):
        u, v = factors(j)
        for part, right in enumerate(paired(u)):
            forward_mem[core, j, part] = outer(v, right)
        give_forward(j).start()

    def with_turned(x):
        turned = []
        for k in range(0, x.shape[0], rows):
            turned += [-x[k + half:k + rows], x[k:k + half]]
        return [x, jnp.concatenate(turned, axis=0)]

    def apply(lhs, weight):
        return jnp.dot(lhs, weight.reshape(-1, width), preferred_element_type=F32)

    def gathered(block):
        return apply(
            jnp.concatenate(with_turned(block.reshape(2 * rows, width)), axis=1), forward_mem[core, me_block]
        )

    total = None
    for k in [0, 1, *range(2, n)]:
        me_block = lax.rem(me + k, n) if k != 1 else twin
        if k >= 2:
            me_block = 2 * chip_order[k // 2] + k % 2
        if k == 0:
            block = up_own[...]
        else:
            arrived(up_all.at[me_block], gather_rsem.at[me_block])
            block = up_all[me_block]
        term = gathered(block)
        total = term if total is None else total + term
    total = total.reshape(2, rows, width)
    up_send[0] = total.astype(BF16)

    @pl.when(has_above)
    def _():
        for q in far_chips:
            for h in range(2):
                up_step0(q, h).start()

    first_half, second_half = total[0], total[1]
    first_term[core] = jnp.where(core == 0, first_half, second_half)
    twin_term[...] = jnp.where(core == 0, second_half, first_half)
    give_term.start()

    def spread(blocks):
        sides = []
        for x in blocks:
            sides += with_turned(x)
        return jnp.concatenate(sides, axis=1)

    def send_down(t, out):
        for j in range(n):
            down_send[t, j] = out[j].astype(BF16)

        @pl.when(has_below)
        def _():
            for q in far_chips:
                down_step(t, q).start()

    @pl.when(has_above)
    def _():
        for h in range(2):
            arrived(first_in.at[h], first_rsem.at[h])

    lhs = spread([first_in[0], first_in[1]])
    for j in range(n):
        arrived(backward_mem.at[j, 1 - core], back_rsem.at[j])
    out = [apply(lhs, backward_mem[j]) for j in range(n)]
    for j in range(n):
        base[j] = out[j]
    send_down(0, out)

    for t in range(1, STEPS):
        last = t == STEPS - 1
        if t == 1:
            for j in range(n):
                arrived(forward_mem.at[1 - core, j], forw_rsem.at[j])
            arrived(first_term.at[1 - core], term_rsem)
        total = [first_term[h] for h in range(2)]
        for q in chip_order:

            @pl.when(has_below)
            def _():
                if t == 1:
                    for h in range(2):
                        arrived(up_in.at[0, 2 * q + h], up_rsem0.at[2 * q + h])
                else:
                    arrived(up_in.at[1, pl.ds(2 * q, 2)], up_rsem.at[q])

            lhs = spread([up_in[t - 1, 2 * q], up_in[t - 1, 2 * q + 1]])
            total = [
                total[h] + apply(lhs, forward_mem[h, pl.ds(2 * q, 2)]) for h in range(2)
            ]
        for h in range(2):
            if last:
                up_last_send[h] = total[h].astype(BF16)
            else:
                up_send[t, h] = total[h].astype(BF16)

        @pl.when(has_above)
        def _():
            if last:
                for h in range(2):
                    up_last(h).start()
            else:
                for q in far_chips:
                    up_step1(q).start()

        @pl.when(has_above)
        def _():
            for q in chip_order:
                arrived(down_in.at[t - 1, q], down_rsem.at[t - 1, q])

        blocks = []
        for h in range(2):
            x = down_in[t - 1, chip_order[0], h].astype(F32)
            for q in chip_order[1:]:
                x = x + down_in[t - 1, q, h].astype(F32)
            blocks.append(x.astype(BF16))
        lhs = spread(blocks)
        if not last:
            send_down(t, [base[j] + apply(lhs, backward_mem[j]) for j in range(n)])
        else:
            for k in far_first:
                to = lax.rem(me + k, n)
                down_last_send[to] = (base[to] + apply(lhs, backward_mem[to])).astype(BF16)
                down_last(k).start()
            own_part = base[me] + apply(lhs, backward_mem[me])

    def place(ref, halves):
        for h, x in enumerate(halves):
            for part in range(2):
                ref[0, part, h * half:(h + 1) * half] = x[part * half:(part + 1) * half].astype(BF16)

    halves = []
    for k in range(1, n):
        block = lax.rem(me + k, n)
        arrived(down_last_in.at[block], down_last_rsem.at[block])
    for h in range(2):
        x = down_own[h].astype(F32)
        for q in range(chips):
            block = 2 * q + h
            x = x + jnp.where(block == me, own_part, down_last_in[block].astype(F32))
        halves.append(x)
    place(down_out, halves)

    @pl.when(has_below)
    def _():
        for h in range(2):
            arrived(up_last_in.at[h], up_last_rsem.at[h])

    place(up_out, [up_own[h].astype(F32) + up_last_in[h].astype(F32) for h in range(2)])

    for k in range(1, n):
        gather(k).wait_send()
        down_last(k).wait_send()
    for j in range(n):
        give_backward(j).wait_send()
        give_forward(j).wait_send()
    give_term.wait_send()

    @pl.when(has_below)
    def _():
        for h in range(2):
            first(h).wait_send()
        for t in range(STEPS - 1):
            for q in range(chips):
                down_step(t, q).wait_send()

    @pl.when(has_above)
    def _():
        for q in range(chips):
            for h in range(2):
                up_step0(q, h).wait_send()
            up_step1(q).wait_send()
        for h in range(2):
            up_last(h).wait_send()


def hand_over(up_mem, down_mem, up_out, down_out, sems):
    stores = [
        pltpu.make_async_copy(mem, dst, sems.at[i])
        for i, (mem, dst) in enumerate([(up_mem, up_out), (down_mem, down_out)])
    ]
    for store in stores:
        store.start()
    for store in stores:
        store.wait()


def solution(mesh):
    layers, n = mesh.shape["gz"], mesh.shape["xy"]
    chips = n // 2

    def on_device(up_source, down_source, source_layer, u_factor, v_factor, block_rank):
        _, _, sources, width = up_source.shape
        max_rank = u_factor.shape[4]
        rows = sources
        piece = (rows, width)
        anywhere = pl.BlockSpec(memory_space=pl.ANY)
        hbm = pl.BlockSpec(memory_space=pltpu.HBM)
        vmem = pl.BlockSpec(memory_space=pltpu.VMEM)
        dma = pltpu.SemaphoreType.DMA
        traces = pl.pallas_call(
            functools.partial(kernel, layers, n),
            out_shape=(pltpu.VMEM(up_source.shape, BF16), pltpu.VMEM(down_source.shape, BF16)),
            in_specs=[hbm] * 6,
            out_specs=(vmem, vmem),
            scratch_shapes=[
                pltpu.VMEM((2, sources, width), BF16),
                pltpu.VMEM((2, sources, width), BF16),
                pltpu.VMEM((1, sources), jnp.int32),
                pltpu.SMEM(block_rank.shape, jnp.int32),
                pltpu.VMEM(u_factor.shape[2:], BF16),
                pltpu.VMEM(v_factor.shape[2:], BF16),
                pltpu.VMEM((2, *piece), BF16),
                pltpu.VMEM((2, *piece), BF16),
                pltpu.VMEM((n, 2, *piece), BF16),
                pltpu.VMEM((2, *piece), BF16),
                pltpu.VMEM((2, n, 2, width, width), BF16),
                pltpu.VMEM((n, 2, 2, width, width), BF16),
                pltpu.VMEM((2, *piece), F32),
                pltpu.VMEM(piece, F32),
                pltpu.VMEM((n, *piece), F32),
                pltpu.VMEM((STEPS - 1, n, *piece), BF16),
                pltpu.VMEM((STEPS - 1, 2, *piece), BF16),
                pltpu.VMEM((STEPS - 1, chips, 2, *piece), BF16),
                pltpu.VMEM((STEPS - 1, n, *piece), BF16),
                pltpu.VMEM((2, *piece), BF16),
                pltpu.VMEM((2, *piece), BF16),
                pltpu.VMEM((n, *piece), BF16),
                pltpu.VMEM((n, *piece), BF16),
                dma((4,)), dma((n,)), dma((n,)),
                dma((n,)), dma((n,)),
                dma((2,)), dma((2,)),
                dma((n,)), dma((n,)),
                dma((n,)), dma((n,)),
                dma, dma,
                dma((n,)), dma((n,)),
                dma((chips,)), dma((chips,)),
                dma((2,)), dma((2,)),
                dma((STEPS - 1, chips)), dma((STEPS - 1, chips)),
                dma((n,)), dma((n,)),
            ],
            compiler_params=pltpu.CompilerParams(collective_id=0, has_side_effects=True),
        )(up_source, down_source, source_layer.reshape(1, sources), u_factor, v_factor, block_rank)
        traces = [pltpu.with_memory_space_constraint(x, pltpu.VMEM) for x in traces]
        return pl.pallas_call(
            hand_over,
            out_shape=(
                jax.ShapeDtypeStruct(up_source.shape, BF16),
                jax.ShapeDtypeStruct(down_source.shape, BF16),
            ),
            in_specs=[vmem, vmem],
            out_specs=(anywhere, anywhere),
            scratch_shapes=[dma((2,))],
        )(*traces)

    in_specs = (
        P("gz", None, None, "xy"),
        P("gz", None, None, "xy"),
        P(),
        P("gz", "xy", None, None, None, None),
        P("gz", "xy", None, None, None, None),
        P("gz", "xy", None),
    )
    out_specs = (P("gz", None, None, "xy"), P("gz", None, None, "xy"))
    return jax.shard_map(
        on_device, mesh=mesh, in_specs=in_specs, out_specs=out_specs, check_vma=False
    )
```

```python
import functools

import jax
import jax.numpy as jnp
from jax import lax
from jax.experimental import pallas as pl
from jax.experimental.pallas import tpu as pltpu
from jax.sharding import PartitionSpec as P

STEPS = 3
MESH = pl.DeviceIdType.MESH
F32, BF16 = jnp.float32, jnp.bfloat16
UP, DOWN = 0, 1
LEFT, RIGHT = 0, 1
ORDER = ((UP, DOWN), (UP, DOWN), (UP, DOWN))


def kernel(
    layers, n, up_hbm, down_hbm, layer_hbm, u_hbm, v_hbm, rank_hbm, up_out, down_out,
    layer_ref, rank_ref, own, factors, up_all, first_in, dense, up_base, down_base,
    up_in, up_send, down_in, down_send, up_last_in, up_last_send, down_last_in, down_last_send,
    load_sem, factor_sem, twin_ssem, twin_rsem, gather_ssem, gather_rsem, first_ssem, first_rsem,
    up_ssem, up_rsem, up_last_ssem, up_last_rsem, down_ssem, down_rsem, down_last_ssem, down_last_rsem,
    ready_sem,
):
    layer = lax.axis_index("gz")
    me = lax.axis_index("xy")
    has_above = layer < layers - 1
    has_below = layer > 0
    chips = n // 2
    chip = me // 2
    core = lax.rem(me, 2)
    twin = me + 1 - 2 * core
    _, _, sources, width = own.shape
    half = sources // 2
    rows = 2 * half
    max_rank = factors.shape[4]
    step = max_rank // 4
    chip_order = [lax.rem(chip + k, chips) for k in range(chips)]
    far_chips = chip_order[1:]
    far_first = [*far_chips, chip]

    def remote(src, dst, ssem, rsem, to_layer, to_block):
        return pltpu.make_async_remote_copy(
            src_ref=src, dst_ref=dst, send_sem=ssem, recv_sem=rsem,
            device_id={"gz": to_layer, "xy": to_block}, device_id_type=MESH,
        )

    def arrived(ref, rsem):
        remote(ref, ref, gather_ssem, rsem, layer, me).wait_recv()

    def sent(ref, ssem):
        remote(ref, ref, ssem, twin_rsem, layer, me).wait_send()

    def tell(sem, to_layer, to_block):
        pl.semaphore_signal(
            sem, inc=1, device_id={"gz": to_layer, "xy": to_block}, device_id_type=MESH
        )

    barrier = pltpu.get_barrier_semaphore()

    @pl.when(has_above)
    def _():
        tell(barrier, layer + 1, me)
        tell(barrier, layer + 1, twin)

    for q in far_chips:
        for h in range(2):
            tell(barrier, layer, 2 * q + h)
    tell(barrier, layer, twin)

    def half_of(ref, h):
        return ref.at[0, :, pl.ds(pl.multiple_of(h * half, half), half)]

    load_factors = [
        pltpu.make_async_copy(hbm.at[0, 0], factors.at[core, kind], factor_sem)
        for kind, hbm in ((LEFT, u_hbm), (RIGHT, v_hbm))
    ]
    load_rank = pltpu.make_async_copy(rank_hbm, rank_ref, load_sem.at[0])
    load_layer = pltpu.make_async_copy(layer_hbm, layer_ref, load_sem.at[1])
    load_half = pltpu.make_async_copy(half_of(up_hbm, core), up_all.at[me], load_sem.at[2])
    load_own = [
        pltpu.make_async_copy(hbm.at[0], own.at[kind], load_sem.at[3]) for kind, hbm in ((UP, up_hbm), (DOWN, down_hbm))
    ]
    for load in (*load_factors, load_rank, load_layer, load_half, *load_own):
        load.start()

    @pl.when(jnp.logical_not(has_below))
    def _():
        up_in[...] = jnp.zeros_like(up_in)
        up_last_in[...] = jnp.zeros_like(up_last_in)

    @pl.when(jnp.logical_not(has_above))
    def _():
        first_in[...] = jnp.zeros_like(first_in)
        down_in[...] = jnp.zeros_like(down_in)

    pl.semaphore_wait(barrier, n - 1 + jnp.where(has_below, 2, 0))

    def gather(to, h):
        return remote(half_of(up_hbm, h), up_all.at[me], gather_ssem, gather_rsem.at[chip], layer, to)

    def first(h):
        return remote(
            half_of(down_hbm, h), first_in.at[core], first_ssem, first_rsem, layer - 1, 2 * chip + h
        )

    def give_left():
        slot = factors.at[core, LEFT]
        return remote(slot, slot, twin_ssem, twin_rsem, layer, twin)

    def give_right():
        return remote(v_hbm.at[0, 0], factors.at[core, RIGHT], twin_ssem, twin_rsem, layer, twin)

    def up_step(t, q):
        return remote(
            up_send.at[t], up_in.at[t, pl.ds(2 * chip, 2)], up_ssem, up_rsem.at[t, chip], layer + 1, 2 * q + core
        )

    def up_last(h):
        return remote(
            up_last_send.at[h], up_last_in.at[core], up_last_ssem, up_last_rsem, layer + 1, 2 * chip + h
        )

    def down_step(t, q):
        return remote(
            down_send.at[t, pl.ds(2 * q, 2)], down_in.at[t, chip], down_ssem, down_rsem.at[t],
            layer - 1, 2 * q + core,
        )

    def slot_of(to):
        return lax.rem(to - me + n, n) - 1

    def down_last(to):
        slot = slot_of(to)
        return remote(
            down_last_send.at[slot], down_last_in.at[n - 2 - slot], down_last_ssem, down_last_rsem, layer, to
        )

    @pl.when(has_below)
    def _():
        for h in range(2):
            first(h).start()
        tell(ready_sem, layer - 1, me)

    for q in far_chips:
        for h in range(2):
            gather(2 * q + h, h).start()
    gather(twin, 1 - core).start()
    give_right().start()

    def turned(x):
        middle = x.shape[0] // 2
        return jnp.concatenate([-x[middle:], x[:middle]], axis=0)

    def spread(blocks):
        return jnp.concatenate([side for x in blocks for side in (x, turned(x))], axis=1)

    def dot(lhs, weights):
        return jnp.dot(lhs, weights, preferred_element_type=F32)

    def stacked(row, kind, j):
        return factors[row, kind, j].reshape(2 * max_rank, width)

    def outer(a, b):
        pair = jnp.concatenate(
            [
                jnp.concatenate([b[:max_rank], -b[max_rank:]], axis=0),
                jnp.concatenate([b[max_rank:], b[:max_rank]], axis=0),
            ],
            axis=1,
        )
        product = lax.dot_general(a, pair, (((0,), (0,)), ((), ())), preferred_element_type=F32).astype(BF16)
        return product[:, :width], product[:, width:]

    def make_dense(row, kind):
        first_kind, second_kind = (RIGHT, LEFT) if kind == UP else (LEFT, RIGHT)
        for j in range(n):
            for part, x in enumerate(outer(stacked(row, first_kind, j), stacked(row, second_kind, j))):
                dense[row, kind, j, part] = x

    pltpu.make_async_copy(factors.at[core], factors.at[core], factor_sem).wait()
    load_rank.wait()
    for j in range(n):
        for part in range(2):
            for g in range(4):
                spot = pl.ds(g * step, step)
                piece = factors[core, LEFT, j, part, spot]
                factors[core, LEFT, j, part, spot] = jnp.where(
                    rank_ref[0, 0, j] > g, piece, jnp.zeros_like(piece)
                )
    give_left().start()
    make_dense(core, UP)
    make_dense(core, DOWN)

    load_layer.wait()
    square = (sources, sources)
    diagonal = lax.broadcasted_iota(jnp.int32, square, 0) == lax.broadcasted_iota(jnp.int32, square, 1)
    source_layer = jnp.sum(
        jnp.where(diagonal, jnp.broadcast_to(layer_ref[...], square), 0), axis=1, keepdims=True
    )
    source_layer = jnp.broadcast_to(source_layer, (sources, width))
    my_half = jnp.where(core == 0, source_layer[:half], source_layer[half:])
    my_half = jnp.concatenate([my_half, my_half], axis=0)
    load_half.wait()
    pltpu.make_async_copy(own, own, load_sem.at[3]).wait()

    arrived(factors.at[1 - core], twin_rsem)
    make_dense(1 - core, UP)
    make_dense(1 - core, DOWN)

    def rise(t):
        last = t == STEPS - 1
        total = [up_base[h] if t > 0 else None for h in range(2)]
        for i, q in enumerate(chip_order):
            if t == 0:
                pair = up_all.at[pl.ds(2 * q, 2)]
                arrived(up_all.at[twin] if i == 0 else pair, gather_rsem.at[q])
            else:
                pair = up_in.at[t - 1, pl.ds(2 * q, 2)]

                @pl.when(has_below)
                def _():
                    arrived(pair, up_rsem.at[t - 1, q])

            lhs = spread([pair[h].reshape(rows, width) for h in range(2)])
            for h in range(2):
                term = dot(lhs, dense[h, UP, pl.ds(2 * q, 2)].reshape(4 * width, width))
                total[h] = term if total[h] is None else total[h] + term
        for h in range(2):
            if t == 0:
                total[h] = jnp.where(layer >= my_half, total[h], 0.0)
            if last:
                up_last_send[h] = total[h].astype(BF16)
            else:
                up_send[t, h] = total[h].astype(BF16)

        @pl.when(has_above)
        def _():
            if t == 0:
                pl.semaphore_wait(ready_sem, 1)
            if last:
                for h in range(2):
                    up_last(h).start()
            else:
                for q in far_first:
                    up_step(t, q).start()

        if t == 0:
            for h in range(2):
                up_base[h] = total[h]

    def fall(t):
        last = t == STEPS - 1

        @pl.when(has_above)
        def _():
            if t == 0:
                arrived(first_in, first_rsem)
            else:
                arrived(down_in.at[t - 1], down_rsem.at[t - 1])

        blocks = []
        for h in range(2):
            if t == 0:
                x = jnp.where(layer + 1 <= my_half, first_in[h].reshape(rows, width).astype(F32), 0.0)
            else:
                x = down_in[t - 1, 0, h].astype(F32)
                for q in range(1, chips):
                    x = x + down_in[t - 1, q, h].astype(F32)
            blocks.append(x.astype(BF16))
        lhs = spread(blocks)

        def back(j):
            out = dot(
                lhs, jnp.concatenate([dense[h, DOWN, j].reshape(2 * width, width) for h in range(2)], axis=0)
            )
            if t == 0:
                down_base[j] = out
            else:
                out = down_base[j] + out
            return out

        if last:
            for q in far_chips:
                for h in range(2):
                    down_last_send[slot_of(2 * q + h)] = back(2 * q + h).astype(BF16)
            for q in far_chips:
                for h in range(2):
                    down_last(2 * q + h).start()
            down_last_send[slot_of(twin)] = back(twin).astype(BF16)
            mine = back(me)
            down_last(twin).start()
            return mine
        for q in far_first:
            for h in range(2):
                down_send[t, 2 * q + h] = back(2 * q + h).astype(BF16)

        @pl.when(has_below)
        def _():
            for q in far_first:
                down_step(t, q).start()
        return None

    for t, order in enumerate(ORDER):
        for which in order:
            if which == UP:
                rise(t)
            else:
                mine = fall(t)

    def active(kind, keep):
        return [jnp.where(keep, own[kind, part].astype(F32), 0.0) for part in range(2)]

    def place(ref, start, halves):
        for h, x in enumerate(halves):
            for part in range(2):
                spot = pl.ds(h * half, half)
                ref[0, part, spot] = (
                    start[part][h * half:(h + 1) * half] + x[part * half:(part + 1) * half]
                ).astype(BF16)

    def finish_up():
        @pl.when(has_below)
        def _():
            arrived(up_last_in, up_last_rsem)

        place(up_out, active(UP, layer >= source_layer), [up_last_in[h].astype(F32) for h in range(2)])

    def finish_down():
        arrived(down_last_in, down_last_rsem)
        same, other = mine, 0.0
        for k in range(n - 1):
            x = down_last_in[k].astype(F32)
            if k % 2:
                same = same + x
            else:
                other = other + x
        place(
            down_out, active(DOWN, layer <= source_layer),
            [jnp.where(core == 0, same, other), jnp.where(core == 0, other, same)],
        )

    finish_down()
    finish_up()

    sent(factors.at[core], twin_ssem)
    sent(down_last_send, gather_ssem)
    sent(down_last_send, down_last_ssem)

    @pl.when(has_below)
    def _():
        sent(first_in, first_ssem)
        sent(down_send, down_ssem)

    @pl.when(has_above)
    def _():
        sent(up_in, up_ssem)
        sent(up_last_send, up_last_ssem)


def hand_over(up_mem, down_mem, up_out, down_out, sems):
    stores = [
        pltpu.make_async_copy(mem, dst, sems.at[i])
        for i, (mem, dst) in enumerate([(up_mem, up_out), (down_mem, down_out)])
    ]
    for store in stores:
        store.start()
    for store in stores:
        store.wait()


def solution(mesh):
    layers, n = mesh.shape["gz"], mesh.shape["xy"]
    chips = n // 2

    def on_device(up_source, down_source, source_layer, u_factor, v_factor, block_rank):
        _, _, sources, width = up_source.shape
        half = sources // 2
        piece = (2 * half, width)
        anywhere = pl.BlockSpec(memory_space=pl.ANY)
        hbm = pl.BlockSpec(memory_space=pltpu.HBM)
        vmem = pl.BlockSpec(memory_space=pltpu.VMEM)
        dma = pltpu.SemaphoreType.DMA
        traces = pl.pallas_call(
            functools.partial(kernel, layers, n),
            out_shape=(pltpu.VMEM(up_source.shape, BF16), pltpu.VMEM(down_source.shape, BF16)),
            in_specs=[hbm] * 6,
            out_specs=(vmem, vmem),
            scratch_shapes=[
                pltpu.VMEM((1, sources), jnp.int32),
                pltpu.SMEM(block_rank.shape, jnp.int32),
                pltpu.VMEM((2, *up_source.shape[1:]), BF16),
                pltpu.VMEM((2, 2, *u_factor.shape[2:]), BF16),
                pltpu.VMEM((n, 2, half, width), BF16),
                pltpu.VMEM((2, 2, half, width), BF16),
                pltpu.VMEM((2, 2, n, 2, width, width), BF16),
                pltpu.VMEM((2, *piece), F32),
                pltpu.VMEM((n, *piece), F32),
                pltpu.VMEM((STEPS - 1, n, *piece), BF16),
                pltpu.VMEM((STEPS - 1, 2, *piece), BF16),
                pltpu.VMEM((STEPS - 1, chips, 2, *piece), BF16),
                pltpu.VMEM((STEPS - 1, n, *piece), BF16),
                pltpu.VMEM((2, *piece), BF16),
                pltpu.VMEM((2, *piece), BF16),
                pltpu.VMEM((n - 1, *piece), BF16),
                pltpu.VMEM((n - 1, *piece), BF16),
                dma((4,)), dma,
                dma, dma,
                dma, dma((chips,)),
                dma, dma,
                dma, dma((STEPS - 1, chips)),
                dma, dma,
                dma, dma((STEPS - 1,)),
                dma, dma,
                pltpu.SemaphoreType.REGULAR,
            ],
            compiler_params=pltpu.CompilerParams(collective_id=0, has_side_effects=True),
        )(up_source, down_source, source_layer.reshape(1, sources), u_factor, v_factor, block_rank)
        traces = [pltpu.with_memory_space_constraint(x, pltpu.VMEM) for x in traces]
        return pl.pallas_call(
            hand_over,
            out_shape=(
                jax.ShapeDtypeStruct(up_source.shape, BF16),
                jax.ShapeDtypeStruct(down_source.shape, BF16),
            ),
            in_specs=[vmem, vmem],
            out_specs=(anywhere, anywhere),
            scratch_shapes=[dma((2,))],
        )(*traces)

    in_specs = (
        P("gz", None, None, "xy"),
        P("gz", None, None, "xy"),
        P(),
        P("gz", "xy", None, None, None, None),
        P("gz", "xy", None, None, None, None),
        P("gz", "xy", None),
    )
    out_specs = (P("gz", None, None, "xy"), P("gz", None, None, "xy"))
    return jax.shard_map(
        on_device, mesh=mesh, in_specs=in_specs, out_specs=out_specs, check_vma=False
    )
```

```python
import functools

import jax
import jax.numpy as jnp
from jax import lax
from jax.experimental import pallas as pl
from jax.experimental.pallas import tpu as pltpu
from jax.sharding import PartitionSpec as P

STEPS = 3
MESH = pl.DeviceIdType.MESH
F32, BF16 = jnp.float32, jnp.bfloat16
UP, DOWN = 0, 1
LEFT, RIGHT = 0, 1
ORDER = ((UP, DOWN), (UP, DOWN), (UP, DOWN))


def kernel(
    layers, n, up_hbm, down_hbm, layer_hbm, u_hbm, v_hbm, rank_hbm, up_out, down_out,
    layer_ref, rank_ref, own, factors, up_all, first_in, dense, up_base, down_base,
    up_in, up_send, down_in, down_send, up_last_in, up_last_send, down_last_in, down_last_send,
    load_sem, factor_sem, twin_ssem, twin_rsem, gather_ssem, gather_rsem, first_ssem, first_rsem,
    up_ssem, up_rsem, up_last_ssem, up_last_rsem, down_ssem, down_rsem, down_last_ssem, down_last_rsem,
    ready_sem,
):
    layer = lax.axis_index("gz")
    me = lax.axis_index("xy")
    has_above = layer < layers - 1
    has_below = layer > 0
    chips = n // 2
    chip = me // 2
    core = lax.rem(me, 2)
    side = lax.rem(core + layer, 2)
    twin = me + 1 - 2 * core
    _, _, sources, width = own.shape
    half = sources // 2
    rows = 2 * half
    max_rank = factors.shape[4]
    step = max_rank // 4
    chip_order = [lax.rem(chip + k, chips) for k in range(chips)]
    far_chips = chip_order[1:]
    far_first = [*far_chips, chip]

    def remote(src, dst, ssem, rsem, to_layer, to_block):
        return pltpu.make_async_remote_copy(
            src_ref=src, dst_ref=dst, send_sem=ssem, recv_sem=rsem,
            device_id={"gz": to_layer, "xy": to_block}, device_id_type=MESH,
        )

    def arrived(ref, rsem):
        remote(ref, ref, gather_ssem, rsem, layer, me).wait_recv()

    def sent(ref, ssem):
        remote(ref, ref, ssem, twin_rsem.at[0], layer, me).wait_send()

    def tell(sem, to_layer, to_block):
        pl.semaphore_signal(
            sem, inc=1, device_id={"gz": to_layer, "xy": to_block}, device_id_type=MESH
        )

    barrier = pltpu.get_barrier_semaphore()

    @pl.when(has_above)
    def _():
        tell(barrier, layer + 1, me)
        tell(barrier, layer + 1, twin)

    for q in far_chips:
        for h in range(2):
            tell(barrier, layer, 2 * q + h)
    tell(barrier, layer, twin)

    def half_of(ref, h):
        return ref.at[0, :, pl.ds(pl.multiple_of(h * half, half), half)]

    load_factors = [
        pltpu.make_async_copy(hbm.at[0, 0], factors.at[core, kind], factor_sem)
        for kind, hbm in ((LEFT, u_hbm), (RIGHT, v_hbm))
    ]
    load_rank = pltpu.make_async_copy(rank_hbm, rank_ref, load_sem.at[0])
    load_layer = pltpu.make_async_copy(layer_hbm, layer_ref, load_sem.at[1])
    load_half = pltpu.make_async_copy(half_of(up_hbm, side), up_all.at[me], load_sem.at[2])
    load_own = [
        pltpu.make_async_copy(hbm.at[0], own.at[kind], load_sem.at[3]) for kind, hbm in ((UP, up_hbm), (DOWN, down_hbm))
    ]
    for load in (*load_factors, load_rank, load_layer, load_half, *load_own):
        load.start()

    hears_up = jnp.logical_and(has_below, has_above)
    feeds_up = layer < layers - 2
    hears_down = [jnp.logical_and(has_below, feeds_up), feeds_up]
    feeds_down = [jnp.logical_and(layer > 1, has_above), jnp.logical_and(has_below, has_above)]

    @pl.when(jnp.logical_not(hears_up))
    def _():
        up_in[...] = jnp.zeros_like(up_in)

    @pl.when(jnp.logical_not(has_below))
    def _():
        up_last_in[...] = jnp.zeros_like(up_last_in)

    @pl.when(jnp.logical_not(has_above))
    def _():
        first_in[...] = jnp.zeros_like(first_in)

    for t in range(STEPS - 1):

        @pl.when(jnp.logical_not(hears_down[t]))
        def _():
            down_in[t] = jnp.zeros_like(down_in[t])

    pl.semaphore_wait(barrier, n - 1 + jnp.where(has_below, 2, 0))

    def gather(to, h):
        return remote(half_of(up_hbm, h), up_all.at[me], gather_ssem, gather_rsem.at[chip], layer, to)

    def first(h):
        return remote(
            half_of(down_hbm, lax.rem(layer + 1 + h, 2)), first_in.at[core], first_ssem, first_rsem, layer - 1, 2 * chip + h
        )

    def group(g):
        return pl.ds(g * chips, chips)

    def give_left(g):
        slot = factors.at[core, LEFT, group(g)]
        return remote(slot, slot, twin_ssem, twin_rsem.at[g], layer, twin)

    def give_right(g):
        return remote(
            v_hbm.at[0, 0, group(g)], factors.at[core, RIGHT, group(g)], twin_ssem, twin_rsem.at[g], layer, twin
        )

    def up_step(t, q):
        return remote(
            up_send.at[t], up_in.at[t, pl.ds(2 * chip, 2)], up_ssem, up_rsem.at[t, chip], layer + 1, 2 * q + 1 - core
        )

    def up_last(h):
        return remote(
            up_last_send.at[h], up_last_in.at[side], up_last_ssem, up_last_rsem, layer + 1, 2 * chip + h
        )

    def down_step(t, q):
        return remote(
            down_send.at[t, pl.ds(2 * q, 2)], down_in.at[t, chip], down_ssem.at[t], down_rsem.at[t],
            layer - 1, 2 * q + 1 - core,
        )

    def slot_of(to):
        return lax.rem(to - me + n, n) - 1

    def down_last(to):
        slot = slot_of(to)
        return remote(
            down_last_send.at[slot], down_last_in.at[n - 2 - slot], down_last_ssem, down_last_rsem, layer, to
        )

    @pl.when(has_below)
    def _():
        for h in range(2):
            first(h).start()
        tell(ready_sem, layer - 1, me)

    for q in far_chips:
        for h in range(2):
            gather(2 * q + h, lax.rem(layer + h, 2)).start()
    gather(twin, 1 - side).start()
    for g in range(2):
        give_right(g).start()

    def turned(x):
        middle = x.shape[0] // 2
        return jnp.concatenate([-x[middle:], x[:middle]], axis=0)

    def spread(blocks):
        return jnp.concatenate([side for x in blocks for side in (x, turned(x))], axis=1)

    def dot(lhs, weights):
        return jnp.dot(lhs, weights, preferred_element_type=F32)

    def stacked(row, kind, j):
        return factors[row, kind, j].reshape(2 * max_rank, width)

    def outer(a, b):
        pair = jnp.concatenate(
            [
                jnp.concatenate([b[:max_rank], -b[max_rank:]], axis=0),
                jnp.concatenate([b[max_rank:], b[:max_rank]], axis=0),
            ],
            axis=1,
        )
        product = lax.dot_general(a, pair, (((0,), (0,)), ((), ())), preferred_element_type=F32).astype(BF16)
        return product[:, :width], product[:, width:]

    def make_dense(row, kind, g):
        first_kind, second_kind = (RIGHT, LEFT) if kind == UP else (LEFT, RIGHT)
        for j in range(g * chips, (g + 1) * chips):
            for part, x in enumerate(outer(stacked(row, first_kind, j), stacked(row, second_kind, j))):
                dense[row, kind, j, part] = x

    pltpu.make_async_copy(factors.at[core], factors.at[core], factor_sem).wait()
    load_rank.wait()
    for j in range(n):
        for part in range(2):
            for g in range(4):
                spot = pl.ds(g * step, step)
                piece = factors[core, LEFT, j, part, spot]
                factors[core, LEFT, j, part, spot] = jnp.where(
                    rank_ref[0, 0, j] > g, piece, jnp.zeros_like(piece)
                )
    for g in range(2):
        give_left(g).start()
    for g in range(2):
        make_dense(core, UP, g)
        make_dense(core, DOWN, g)

    load_layer.wait()
    square = (sources, sources)
    diagonal = lax.broadcasted_iota(jnp.int32, square, 0) == lax.broadcasted_iota(jnp.int32, square, 1)
    source_layer = jnp.sum(
        jnp.where(diagonal, jnp.broadcast_to(layer_ref[...], square), 0), axis=1, keepdims=True
    )
    source_layer = jnp.broadcast_to(source_layer, (sources, width))
    my_half = jnp.where(side == 0, source_layer[:half], source_layer[half:])
    my_half = jnp.concatenate([my_half, my_half], axis=0)
    load_half.wait()
    pltpu.make_async_copy(own, own, load_sem.at[3]).wait()

    for g in range(2):
        arrived(factors.at[1 - core, :, group(g)], twin_rsem.at[g])
        make_dense(1 - core, UP, g)
        if g == 0:
            make_dense(1 - core, DOWN, g)

    def rise(t):
        last = t == STEPS - 1
        total = [up_base[h] if t > 0 else None for h in range(2)]
        for i, q in enumerate(chip_order):
            if t == 0:
                pair = up_all.at[pl.ds(2 * q, 2)]
                arrived(up_all.at[twin] if i == 0 else pair, gather_rsem.at[q])
            else:
                pair = up_in.at[t - 1, pl.ds(2 * q, 2)]

                @pl.when(hears_up)
                def _():
                    arrived(pair, up_rsem.at[t - 1, q])

            lhs = spread([pair[h].reshape(rows, width) for h in range(2)])
            for h in range(2):
                term = dot(lhs, dense[h, UP, pl.ds(2 * q, 2)].reshape(4 * width, width))
                total[h] = term if total[h] is None else total[h] + term
        for h in range(2):
            if t == 0:
                total[h] = jnp.where(layer >= my_half, total[h], 0.0)
            if last:
                up_last_send[h] = total[h].astype(BF16)
            else:
                up_send[t, h] = total[h].astype(BF16)

        if t == 0:

            @pl.when(has_above)
            def _():
                pl.semaphore_wait(ready_sem, 1)

        @pl.when(has_above if last else feeds_up)
        def _():
            if last:
                for h in range(2):
                    up_last(h).start()
            else:
                for q in far_first:
                    up_step(t, q).start()

        if t == 0:
            for h in range(2):
                up_base[h] = total[h]

    def fall(t):
        last = t == STEPS - 1
        if t == 0:
            make_dense(1 - core, DOWN, 1)

        @pl.when(has_above if t == 0 else hears_down[t - 1])
        def _():
            if t == 0:
                arrived(first_in, first_rsem)
            else:
                arrived(down_in.at[t - 1], down_rsem.at[t - 1])

        blocks = []
        for h in range(2):
            if t == 0:
                x = jnp.where(layer + 1 <= my_half, first_in[h].reshape(rows, width).astype(F32), 0.0)
            else:
                x = down_in[t - 1, 0, h].astype(F32)
                for q in range(1, chips):
                    x = x + down_in[t - 1, q, h].astype(F32)
            blocks.append(x.astype(BF16))
        lhs = spread(blocks)

        def back(j):
            out = dot(
                lhs, jnp.concatenate([dense[h, DOWN, j].reshape(2 * width, width) for h in range(2)], axis=0)
            )
            if t == 0:
                down_base[j] = out
            else:
                out = down_base[j] + out
            return out

        if last:
            for q in far_chips:
                for h in range(2):
                    down_last_send[slot_of(2 * q + h)] = back(2 * q + h).astype(BF16)
            for q in far_chips:
                for h in range(2):
                    down_last(2 * q + h).start()
            down_last_send[slot_of(twin)] = back(twin).astype(BF16)
            mine = back(me)
            down_last(twin).start()
            return mine
        for q in far_first:
            for h in range(2):
                down_send[t, 2 * q + h] = back(2 * q + h).astype(BF16)

        @pl.when(feeds_down[t])
        def _():
            for q in far_first:
                down_step(t, q).start()
        return None

    for t, order in enumerate(ORDER):
        for which in order:
            if which == UP:
                rise(t)
            else:
                mine = fall(t)

    def active(kind, keep):
        return [jnp.where(keep, own[kind, part].astype(F32), 0.0) for part in range(2)]

    def place(ref, start, halves):
        for h, x in enumerate(halves):
            for part in range(2):
                spot = pl.ds(h * half, half)
                ref[0, part, spot] = (
                    start[part][h * half:(h + 1) * half] + x[part * half:(part + 1) * half]
                ).astype(BF16)

    def finish_up():
        @pl.when(has_below)
        def _():
            arrived(up_last_in, up_last_rsem)

        place(up_out, active(UP, layer >= source_layer), [up_last_in[h].astype(F32) for h in range(2)])

    def finish_down():
        arrived(down_last_in, down_last_rsem)
        same, other = mine, 0.0
        for k in range(n - 1):
            x = down_last_in[k].astype(F32)
            if k % 2:
                same = same + x
            else:
                other = other + x
        place(
            down_out, active(DOWN, layer <= source_layer),
            [jnp.where(side == 0, same, other), jnp.where(side == 0, other, same)],
        )

    finish_down()
    finish_up()

    sent(factors.at[core], twin_ssem)
    sent(down_last_send, gather_ssem)
    sent(down_last_send, down_last_ssem)

    @pl.when(has_below)
    def _():
        sent(first_in, first_ssem)

    for t in range(STEPS - 1):

        @pl.when(feeds_down[t])
        def _():
            sent(down_send.at[t], down_ssem.at[t])

    @pl.when(feeds_up)
    def _():
        sent(up_in, up_ssem)

    @pl.when(has_above)
    def _():
        sent(up_last_send, up_last_ssem)


def hand_over(up_mem, down_mem, up_out, down_out, sems):
    stores = [
        pltpu.make_async_copy(mem, dst, sems.at[i])
        for i, (mem, dst) in enumerate([(up_mem, up_out), (down_mem, down_out)])
    ]
    for store in stores:
        store.start()
    for store in stores:
        store.wait()


def solution(mesh):
    layers, n = mesh.shape["gz"], mesh.shape["xy"]
    chips = n // 2

    def on_device(up_source, down_source, source_layer, u_factor, v_factor, block_rank):
        _, _, sources, width = up_source.shape
        half = sources // 2
        piece = (2 * half, width)
        anywhere = pl.BlockSpec(memory_space=pl.ANY)
        hbm = pl.BlockSpec(memory_space=pltpu.HBM)
        vmem = pl.BlockSpec(memory_space=pltpu.VMEM)
        dma = pltpu.SemaphoreType.DMA
        traces = pl.pallas_call(
            functools.partial(kernel, layers, n),
            out_shape=(pltpu.VMEM(up_source.shape, BF16), pltpu.VMEM(down_source.shape, BF16)),
            in_specs=[hbm] * 6,
            out_specs=(vmem, vmem),
            scratch_shapes=[
                pltpu.VMEM((1, sources), jnp.int32),
                pltpu.SMEM(block_rank.shape, jnp.int32),
                pltpu.VMEM((2, *up_source.shape[1:]), BF16),
                pltpu.VMEM((2, 2, *u_factor.shape[2:]), BF16),
                pltpu.VMEM((n, 2, half, width), BF16),
                pltpu.VMEM((2, 2, half, width), BF16),
                pltpu.VMEM((2, 2, n, 2, width, width), BF16),
                pltpu.VMEM((2, *piece), F32),
                pltpu.VMEM((n, *piece), F32),
                pltpu.VMEM((STEPS - 1, n, *piece), BF16),
                pltpu.VMEM((STEPS - 1, 2, *piece), BF16),
                pltpu.VMEM((STEPS - 1, chips, 2, *piece), BF16),
                pltpu.VMEM((STEPS - 1, n, *piece), BF16),
                pltpu.VMEM((2, *piece), BF16),
                pltpu.VMEM((2, *piece), BF16),
                pltpu.VMEM((n - 1, *piece), BF16),
                pltpu.VMEM((n - 1, *piece), BF16),
                dma((4,)), dma,
                dma, dma((2,)),
                dma, dma((chips,)),
                dma, dma,
                dma, dma((STEPS - 1, chips)),
                dma, dma,
                dma((STEPS - 1,)), dma((STEPS - 1,)),
                dma, dma,
                pltpu.SemaphoreType.REGULAR,
            ],
            compiler_params=pltpu.CompilerParams(collective_id=0, has_side_effects=True),
        )(up_source, down_source, source_layer.reshape(1, sources), u_factor, v_factor, block_rank)
        traces = [pltpu.with_memory_space_constraint(x, pltpu.VMEM) for x in traces]
        return pl.pallas_call(
            hand_over,
            out_shape=(
                jax.ShapeDtypeStruct(up_source.shape, BF16),
                jax.ShapeDtypeStruct(down_source.shape, BF16),
            ),
            in_specs=[vmem, vmem],
            out_specs=(anywhere, anywhere),
            scratch_shapes=[dma((2,))],
        )(*traces)

    in_specs = (
        P("gz", None, None, "xy"),
        P("gz", None, None, "xy"),
        P(),
        P("gz", "xy", None, None, None, None),
        P("gz", "xy", None, None, None, None),
        P("gz", "xy", None),
    )
    out_specs = (P("gz", None, None, "xy"), P("gz", None, None, "xy"))
    return jax.shard_map(
        on_device, mesh=mesh, in_specs=in_specs, out_specs=out_specs, check_vma=False
    )
```

```python
import functools

import jax
import jax.numpy as jnp
from jax import lax
from jax.experimental import pallas as pl
from jax.experimental.pallas import tpu as pltpu
from jax.sharding import PartitionSpec as P

STEPS = 3
MESH = pl.DeviceIdType.MESH
F32, BF16 = jnp.float32, jnp.bfloat16
UP, DOWN = 0, 1
LEFT, RIGHT = 0, 1


def kernel(
    layers, n, up_hbm, down_hbm, layer_hbm, u_hbm, v_hbm, rank_hbm, up_out, down_out,
    layer_ref, rank_ref, own, factors, up_all, first_in, dense, up_base, down_base,
    up_in, up_send, down_in, down_send, up_last_send, last, mine,
    load_sem, factor_sem, twin_ssem, twin_rsem, gather_ssem, gather_rsem, first_rsem,
    up_ssem, up_rsem, up_last_rsem, down_ssem, down_rsem, down_last_rsem, ready_sem,
):
    layer = lax.axis_index("gz")
    me = lax.axis_index("xy")
    has_above = layer < layers - 1
    has_below = layer > 0
    chips = n // 2
    chip = me // 2
    core = lax.rem(me, 2)
    side = lax.rem(core + layer, 2)
    twin = me + 1 - 2 * core
    _, _, sources, width = own.shape
    half = sources // 2
    rows = 2 * half
    max_rank = factors.shape[4]
    step = max_rank // 4
    chip_order = [lax.rem(chip + k, chips) for k in range(chips)]
    far_chips = chip_order[1:]
    far_first = [*far_chips, chip]
    inner = (STEPS - 1) * n
    last_in, last_send = last.at[0], last.at[1]

    def remote(src, dst, ssem, rsem, to_layer, to_block):
        return pltpu.make_async_remote_copy(
            src_ref=src, dst_ref=dst, send_sem=ssem, recv_sem=rsem,
            device_id={"gz": to_layer, "xy": to_block}, device_id_type=MESH,
        )

    def arrived(ref, rsem):
        remote(ref, ref, gather_ssem, rsem, layer, me).wait_recv()

    def sent(ref, ssem):
        remote(ref, ref, ssem, twin_rsem.at[0], layer, me).wait_send()

    def tell(sem, to_layer, to_block):
        pl.semaphore_signal(
            sem, inc=1, device_id={"gz": to_layer, "xy": to_block}, device_id_type=MESH
        )

    barrier = pltpu.get_barrier_semaphore()

    @pl.when(has_above)
    def _():
        tell(barrier, layer + 1, me)
        tell(barrier, layer + 1, twin)

    for q in far_chips:
        for h in range(2):
            tell(barrier, layer, 2 * q + h)
    tell(barrier, layer, twin)

    def half_of(ref, h):
        return ref.at[0, :, pl.ds(pl.multiple_of(h * half, half), half)]

    load_factors = [
        pltpu.make_async_copy(hbm.at[0, 0], factors.at[core, kind], factor_sem)
        for kind, hbm in ((LEFT, u_hbm), (RIGHT, v_hbm))
    ]
    load_rank = pltpu.make_async_copy(rank_hbm, rank_ref, load_sem.at[0])
    load_layer = pltpu.make_async_copy(layer_hbm, layer_ref, load_sem.at[1])
    load_own = [
        pltpu.make_async_copy(hbm.at[0], own.at[kind], load_sem.at[2]) for kind, hbm in ((UP, up_hbm), (DOWN, down_hbm))
    ]
    for load in (*load_factors, load_rank, load_layer, *load_own):
        load.start()

    hears_up = jnp.logical_and(has_below, has_above)
    feeds_up = layer < layers - 2
    hears_down = [jnp.logical_and(has_below, feeds_up), feeds_up]
    feeds_down = [jnp.logical_and(layer > 1, has_above), jnp.logical_and(has_below, has_above)]

    @pl.when(jnp.logical_not(hears_up))
    def _():
        up_in[:inner] = jnp.zeros_like(up_in[:inner])

    @pl.when(jnp.logical_not(has_below))
    def _():
        up_in[inner:] = jnp.zeros_like(up_in[inner:])

    @pl.when(jnp.logical_not(has_above))
    def _():
        first_in[...] = jnp.zeros_like(first_in)

    for t in range(STEPS - 1):

        @pl.when(jnp.logical_not(hears_down[t]))
        def _():
            down_in[t] = jnp.zeros_like(down_in[t])

    pl.semaphore_wait(barrier, n - 1 + jnp.where(has_below, 2, 0))

    def gather(to, h):
        return remote(half_of(up_hbm, h), up_all.at[me], gather_ssem, gather_rsem.at[chip], layer, to)

    def first(h):
        return remote(
            half_of(down_hbm, lax.rem(layer + 1 + h, 2)), first_in.at[core], down_ssem, first_rsem, layer - 1, 2 * chip + h
        )

    def group(g):
        return pl.ds(g * chips, chips)

    def give_left(g):
        slot = factors.at[core, LEFT, group(g)]
        return remote(slot, slot, twin_ssem, twin_rsem.at[g], layer, twin)

    def give_right(g):
        return remote(
            v_hbm.at[0, 0, group(g)], factors.at[core, RIGHT, group(g)], twin_ssem, twin_rsem.at[g], layer, twin
        )

    def up_step(t, q):
        return remote(
            up_send.at[t], up_in.at[pl.ds(t * n + 2 * chip, 2)], up_ssem, up_rsem.at[t, chip], layer + 1, 2 * q + 1 - core
        )

    def up_last(h):
        return remote(
            up_last_send.at[h], up_in.at[inner + side], up_ssem, up_last_rsem, layer + 1, 2 * chip + h
        )

    def down_step(t, q, h):
        return remote(
            down_send.at[t * n + 2 * q + h], down_in.at[t, chip, h], down_ssem, down_rsem.at[t, h],
            layer - 1, 2 * q + 1 - core,
        )

    def slot_of(to):
        return lax.rem(to - me + n, n) - 1

    def down_last(to):
        slot = slot_of(to)
        return remote(
            last_send.at[slot], last_in.at[n - 2 - slot], gather_ssem, down_last_rsem, layer, to
        )

    @pl.when(has_below)
    def _():
        for h in range(2):
            first(h).start()
        tell(ready_sem, layer - 1, me)

    for q in far_chips:
        for h in range(2):
            gather(2 * q + h, lax.rem(layer + h, 2)).start()
    gather(twin, 1 - side).start()
    for g in range(2):
        give_right(g).start()

    def turned(x):
        middle = x.shape[0] // 2
        return jnp.concatenate([-x[middle:], x[:middle]], axis=0)

    def spread(blocks):
        return jnp.concatenate([side for x in blocks for side in (x, turned(x))], axis=1)

    def dot(lhs, weights):
        return jnp.dot(lhs, weights, preferred_element_type=F32)

    def stacked(row, kind, j):
        return factors[row, kind, j].reshape(2 * max_rank, width)

    def outer(a, b):
        pair = jnp.concatenate(
            [
                jnp.concatenate([b[:max_rank], -b[max_rank:]], axis=0),
                jnp.concatenate([b[max_rank:], b[:max_rank]], axis=0),
            ],
            axis=1,
        )
        product = lax.dot_general(a, pair, (((0,), (0,)), ((), ())), preferred_element_type=F32).astype(BF16)
        return product[:, :width], product[:, width:]

    def make_dense(row, kind, g):
        first_kind, second_kind = (RIGHT, LEFT) if kind == UP else (LEFT, RIGHT)
        for j in range(g * chips, (g + 1) * chips):
            for part, x in enumerate(outer(stacked(row, first_kind, j), stacked(row, second_kind, j))):
                dense[row, kind, j, part] = x

    pltpu.make_async_copy(factors.at[core], factors.at[core], factor_sem).wait()
    load_rank.wait()
    for j in range(n):
        for part in range(2):
            for g in range(4):
                spot = pl.ds(g * step, step)
                piece = factors[core, LEFT, j, part, spot]
                factors[core, LEFT, j, part, spot] = jnp.where(
                    rank_ref[0, 0, j] > g, piece, jnp.zeros_like(piece)
                )
    for g in range(2):
        give_left(g).start()
    for g in range(2):
        make_dense(core, UP, g)
        make_dense(core, DOWN, g)

    load_layer.wait()
    square = (sources, sources)
    diagonal = lax.broadcasted_iota(jnp.int32, square, 0) == lax.broadcasted_iota(jnp.int32, square, 1)
    source_layer = jnp.sum(
        jnp.where(diagonal, jnp.broadcast_to(layer_ref[...], square), 0), axis=1, keepdims=True
    )
    source_layer = jnp.broadcast_to(source_layer, (sources, width))
    my_half = jnp.where(side == 0, source_layer[:half], source_layer[half:])
    my_half = jnp.concatenate([my_half, my_half], axis=0)
    pltpu.make_async_copy(own, own, load_sem.at[2]).wait()
    up_all[me] = jnp.where(side == 0, own[UP, :, :half], own[UP, :, half:])

    for g in range(2):
        arrived(factors.at[1 - core, :, group(g)], twin_rsem.at[g])
        make_dense(1 - core, UP, g)
        if g == 0:
            make_dense(1 - core, DOWN, g)

    def send_up(t):
        is_last = t == STEPS - 1

        @pl.when(has_above if is_last else feeds_up)
        def _():
            if is_last:
                for h in range(2):
                    up_last(h).start()
            else:
                for q in far_first:
                    up_step(t, q).start()

    def rise(t):
        is_last = t == STEPS - 1
        total = [up_base[h] if t > 0 else None for h in range(2)]
        for i, q in enumerate(chip_order if t == 0 else chip_order):
            if t == 0:
                pair = up_all.at[pl.ds(2 * q, 2)]
                arrived(up_all.at[twin] if i == 0 else pair, gather_rsem.at[q])
            else:
                pair = up_in.at[pl.ds((t - 1) * n + 2 * q, 2)]

                @pl.when(hears_up)
                def _():
                    arrived(pair, up_rsem.at[t - 1, q])

            lhs = spread([pair[h].reshape(rows, width) for h in range(2)])
            for h in range(2):
                term = dot(lhs, dense[h, UP, pl.ds(2 * q, 2)].reshape(4 * width, width))
                total[h] = term if total[h] is None else total[h] + term
        for h in range(2):
            if t == 0:
                total[h] = jnp.where(layer >= my_half, total[h], 0.0)
            if is_last:
                up_last_send[h] = total[h].astype(BF16)
            else:
                up_send[t, h] = total[h].astype(BF16)

        if t == 0:

            @pl.when(has_above)
            def _():
                pl.semaphore_wait(ready_sem, 1)

        if t == 0:
            for h in range(2):
                up_base[h] = total[h]
        send_up(t)

    def fall(t):
        is_last = t == STEPS - 1
        if t == 0:
            make_dense(1 - core, DOWN, 1)

        if t == 0:

            @pl.when(has_above)
            def _():
                arrived(first_in, first_rsem)

        lhs = []
        blocks = [2 * q + h for q in far_first for h in range(2)]
        partial = {}
        for h in range(2):
            if t == 0:
                x = jnp.where(layer + 1 <= my_half, first_in[h].reshape(rows, width).astype(F32), 0.0)
            else:

                @pl.when(hears_down[t - 1])
                def _():
                    arrived(down_in.at[t - 1, :, h], down_rsem.at[t - 1, h])

                x = down_in[t - 1, 0, h].astype(F32)
                for q in range(1, chips):
                    x = x + down_in[t - 1, q, h].astype(F32)
            lhs.append(spread([x.astype(BF16)]))
            if t > 0 and h == 0:
                for i, j in enumerate(blocks):
                    partial[i] = down_base[j] + dot(lhs[0], dense[0, DOWN, j].reshape(2 * width, width))

        def back(i):
            j = blocks[i]
            if t == 0:
                out = dot(
                    jnp.concatenate(lhs, axis=1),
                    jnp.concatenate([dense[h, DOWN, j].reshape(2 * width, width) for h in range(2)], axis=0),
                )
                down_base[j] = out
                return out
            return partial[i] + dot(lhs[1], dense[1, DOWN, j].reshape(2 * width, width))

        if is_last:
            for i in range(n - 2):
                last_send[slot_of(blocks[i])] = back(i).astype(BF16)
            for i in range(n - 2):
                down_last(blocks[i]).start()
            near = [back(n - 2), back(n - 1)]
            last_send[slot_of(twin)] = jnp.where(core == 0, near[1], near[0]).astype(BF16)
            down_last(twin).start()
            mine[...] = jnp.where(core == 0, near[0], near[1])
            return
        for i in range(n):
            down_send[t * n + blocks[i]] = back(i).astype(BF16)

        @pl.when(feeds_down[t])
        def _():
            for q in far_first:
                for h in range(2):
                    down_step(t, q, h).start()

    for t in range(STEPS):
        rise(t)
        fall(t)

    def active(kind, keep):
        return [jnp.where(keep, own[kind, part].astype(F32), 0.0) for part in range(2)]

    def place(ref, start, halves):
        for h, x in enumerate(halves):
            for part in range(2):
                spot = pl.ds(h * half, half)
                ref[0, part, spot] = (
                    start[part][h * half:(h + 1) * half] + x[part * half:(part + 1) * half]
                ).astype(BF16)

    def finish_up():
        @pl.when(has_below)
        def _():
            arrived(up_in.at[pl.ds(inner, 2)], up_last_rsem)

        place(up_out, active(UP, layer >= source_layer), [up_in[inner + h].astype(F32) for h in range(2)])

    def finish_down():
        arrived(last_in, down_last_rsem)
        same, other = mine[...], 0.0
        for k in range(n - 1):
            x = last_in[k].astype(F32)
            if k % 2:
                same = same + x
            else:
                other = other + x
        place(
            down_out, active(DOWN, layer <= source_layer),
            [jnp.where(side == 0, same, other), jnp.where(side == 0, other, same)],
        )

    finish_down()
    finish_up()

    sent(factors.at[core], twin_ssem)
    sent(last, gather_ssem)

    def sent_when(condition, buffer, pieces, ssem):
        @pl.when(condition)
        def _():
            sent(buffer.at[pl.ds(0, pieces)], ssem)

    sent_when(feeds_up, up_in, inner + 2, up_ssem)
    sent_when(layer == layers - 2, up_in, 2, up_ssem)
    sent_when(feeds_down[0], down_send, inner + 2, down_ssem)
    sent_when(jnp.logical_and(layer == 1, has_above), down_send, inner + 2 - n, down_ssem)
    sent_when(jnp.logical_and(has_below, jnp.logical_not(has_above)), down_send, 2, down_ssem)


def hand_over(up_mem, down_mem, up_out, down_out, sems):
    stores = [
        pltpu.make_async_copy(mem, dst, sems.at[i])
        for i, (mem, dst) in enumerate([(up_mem, up_out), (down_mem, down_out)])
    ]
    for store in stores:
        store.start()
    for store in stores:
        store.wait()


def solution(mesh):
    layers, n = mesh.shape["gz"], mesh.shape["xy"]
    chips = n // 2

    def on_device(up_source, down_source, source_layer, u_factor, v_factor, block_rank):
        _, _, sources, width = up_source.shape
        half = sources // 2
        piece = (2 * half, width)
        anywhere = pl.BlockSpec(memory_space=pl.ANY)
        hbm = pl.BlockSpec(memory_space=pltpu.HBM)
        vmem = pl.BlockSpec(memory_space=pltpu.VMEM)
        dma = pltpu.SemaphoreType.DMA
        traces = pl.pallas_call(
            functools.partial(kernel, layers, n),
            out_shape=(pltpu.VMEM(up_source.shape, BF16), pltpu.VMEM(down_source.shape, BF16)),
            in_specs=[hbm] * 6,
            out_specs=(vmem, vmem),
            scratch_shapes=[
                pltpu.VMEM((1, sources), jnp.int32),
                pltpu.SMEM(block_rank.shape, jnp.int32),
                pltpu.VMEM((2, *up_source.shape[1:]), BF16),
                pltpu.VMEM((2, 2, *u_factor.shape[2:]), BF16),
                pltpu.VMEM((n, 2, half, width), BF16),
                pltpu.VMEM((2, 2, half, width), BF16),
                pltpu.VMEM((2, 2, n, 2, width, width), BF16),
                pltpu.VMEM((2, *piece), F32),
                pltpu.VMEM((n, *piece), F32),
                pltpu.VMEM(((STEPS - 1) * n + 2, *piece), BF16),
                pltpu.VMEM((STEPS - 1, 2, *piece), BF16),
                pltpu.VMEM((STEPS - 1, chips, 2, *piece), BF16),
                pltpu.VMEM(((STEPS - 1) * n + 2, *piece), BF16),
                pltpu.VMEM((2, *piece), BF16),
                pltpu.VMEM((2, n - 1, *piece), BF16),
                pltpu.VMEM(piece, F32),
                dma((3,)), dma,
                dma, dma((2,)),
                dma, dma((chips,)), dma,
                dma, dma((STEPS - 1, chips)), dma,
                dma, dma((STEPS - 1, 2)), dma,
                pltpu.SemaphoreType.REGULAR,
            ],
            compiler_params=pltpu.CompilerParams(collective_id=0, has_side_effects=True),
        )(up_source, down_source, source_layer.reshape(1, sources), u_factor, v_factor, block_rank)
        traces = [pltpu.with_memory_space_constraint(x, pltpu.VMEM) for x in traces]
        return pl.pallas_call(
            hand_over,
            out_shape=(
                jax.ShapeDtypeStruct(up_source.shape, BF16),
                jax.ShapeDtypeStruct(down_source.shape, BF16),
            ),
            in_specs=[vmem, vmem],
            out_specs=(anywhere, anywhere),
            scratch_shapes=[dma((2,))],
        )(*traces)

    in_specs = (
        P("gz", None, None, "xy"),
        P("gz", None, None, "xy"),
        P(),
        P("gz", "xy", None, None, None, None),
        P("gz", "xy", None, None, None, None),
        P("gz", "xy", None),
    )
    out_specs = (P("gz", None, None, "xy"), P("gz", None, None, "xy"))
    return jax.shard_map(
        on_device, mesh=mesh, in_specs=in_specs, out_specs=out_specs, check_vma=False
    )
```

```python
import functools

import jax
import jax.numpy as jnp
from jax import lax
from jax.experimental import pallas as pl
from jax.experimental.pallas import tpu as pltpu
from jax.sharding import PartitionSpec as P

STEPS = 3
MESH = pl.DeviceIdType.MESH
F32, BF16 = jnp.float32, jnp.bfloat16
UP, DOWN = 0, 1
LEFT, RIGHT = 0, 1


def kernel(
    layers, n, up_hbm, down_hbm, layer_hbm, u_hbm, v_hbm, rank_hbm, up_out, down_out,
    layer_ref, rank_ref, own, factors, up_all, first_in, dense, up_base, down_base,
    up_in, up_send, down_in, down_send, up_last_send, last, mine,
    load_sem, factor_sem, twin_ssem, twin_rsem, gather_ssem, gather_rsem, first_rsem,
    up_ssem, up_rsem, up_last_rsem, down_ssem, down_rsem, down_last_rsem, ready_sem,
):
    layer = lax.axis_index("gz")
    me = lax.axis_index("xy")
    has_above = layer < layers - 1
    has_below = layer > 0
    chips = n // 2
    chip = me // 2
    core = lax.rem(me, 2)
    side = lax.rem(core + layer, 2)
    twin = me + 1 - 2 * core
    _, _, sources, width = own.shape
    half = sources // 2
    rows = 2 * half
    max_rank = factors.shape[4]
    step = max_rank // 4
    chip_order = [lax.rem(chip + k, chips) for k in range(chips)]
    far_chips = chip_order[1:]
    far_first = [*far_chips, chip]
    inner = (STEPS - 1) * n
    last_in, last_send = last.at[0], last.at[1]

    def remote(src, dst, ssem, rsem, to_layer, to_block):
        return pltpu.make_async_remote_copy(
            src_ref=src, dst_ref=dst, send_sem=ssem, recv_sem=rsem,
            device_id={"gz": to_layer, "xy": to_block}, device_id_type=MESH,
        )

    def arrived(ref, rsem):
        remote(ref, ref, gather_ssem, rsem, layer, me).wait_recv()

    def sent(ref, ssem):
        remote(ref, ref, ssem, twin_rsem.at[0], layer, me).wait_send()

    def tell(sem, to_layer, to_block):
        pl.semaphore_signal(
            sem, inc=1, device_id={"gz": to_layer, "xy": to_block}, device_id_type=MESH
        )

    barrier = pltpu.get_barrier_semaphore()

    @pl.when(has_above)
    def _():
        tell(barrier, layer + 1, me)
        tell(barrier, layer + 1, twin)

    for q in far_chips:
        for h in range(2):
            tell(barrier, layer, 2 * q + h)
    tell(barrier, layer, twin)

    def half_of(ref, h):
        return ref.at[0, :, pl.ds(pl.multiple_of(h * half, half), half)]

    load_factors = [
        pltpu.make_async_copy(hbm.at[0, 0], factors.at[core, kind], factor_sem)
        for kind, hbm in ((LEFT, u_hbm), (RIGHT, v_hbm))
    ]
    load_rank = pltpu.make_async_copy(rank_hbm, rank_ref, load_sem.at[0])
    load_layer = pltpu.make_async_copy(layer_hbm, layer_ref, load_sem.at[1])
    load_own = [
        pltpu.make_async_copy(hbm.at[0], own.at[kind], load_sem.at[2]) for kind, hbm in ((UP, up_hbm), (DOWN, down_hbm))
    ]
    for load in (*load_factors, load_rank, load_layer, *load_own):
        load.start()

    hears_up = jnp.logical_and(has_below, has_above)
    feeds_up = layer < layers - 2
    hears_down = [jnp.logical_and(has_below, feeds_up), feeds_up]
    feeds_down = [jnp.logical_and(layer > 1, has_above), jnp.logical_and(has_below, has_above)]

    @pl.when(jnp.logical_not(hears_up))
    def _():
        up_in[:inner] = jnp.zeros_like(up_in[:inner])

    @pl.when(jnp.logical_not(has_below))
    def _():
        up_in[inner:] = jnp.zeros_like(up_in[inner:])

    @pl.when(jnp.logical_not(has_above))
    def _():
        first_in[...] = jnp.zeros_like(first_in)

    for t in range(STEPS - 1):

        @pl.when(jnp.logical_not(hears_down[t]))
        def _():
            down_in[t] = jnp.zeros_like(down_in[t])

    pl.semaphore_wait(barrier, n - 1 + jnp.where(has_below, 2, 0))

    def gather(to, h):
        return remote(half_of(up_hbm, h), up_all.at[me], gather_ssem, gather_rsem.at[chip], layer, to)

    def first(h):
        return remote(
            half_of(down_hbm, lax.rem(layer + 1 + h, 2)), first_in.at[core], down_ssem, first_rsem, layer - 1, 2 * chip + h
        )

    groups = n
    size = n // groups

    def group(g):
        return pl.ds(g * size, size)

    def give_left(g):
        slot = factors.at[core, LEFT, group(g)]
        return remote(slot, slot, twin_ssem, twin_rsem.at[g], layer, twin)

    def give_right(g):
        return remote(
            v_hbm.at[0, 0, group(g)], factors.at[core, RIGHT, group(g)], twin_ssem, twin_rsem.at[g], layer, twin
        )

    def up_step(t, q):
        return remote(
            up_send.at[t], up_in.at[pl.ds(t * n + 2 * chip, 2)], up_ssem, up_rsem.at[t, chip], layer + 1, 2 * q + 1 - core
        )

    def up_last(h):
        return remote(
            up_last_send.at[h], up_in.at[inner + side], up_ssem, up_last_rsem, layer + 1, 2 * chip + h
        )

    def down_step(t, q, h):
        return remote(
            down_send.at[t * n + 2 * q + h], down_in.at[t, chip, h], down_ssem, down_rsem.at[t, h],
            layer - 1, 2 * q + 1 - core,
        )

    def slot_of(to):
        return lax.rem(to - me + n, n) - 1

    def down_last(to):
        slot = slot_of(to)
        return remote(
            last_send.at[slot], last_in.at[n - 2 - slot], gather_ssem, down_last_rsem, layer, to
        )

    for q in far_chips:
        for h in range(2):
            gather(2 * q + h, lax.rem(layer + h, 2)).start()

    @pl.when(has_below)
    def _():
        for h in range(2):
            first(h).start()
        tell(ready_sem, layer - 1, me)

    gather(twin, 1 - side).start()
    give_right(0).start()

    def turned(x):
        middle = x.shape[0] // 2
        return jnp.concatenate([-x[middle:], x[:middle]], axis=0)

    def spread(blocks):
        return jnp.concatenate([side for x in blocks for side in (x, turned(x))], axis=1)

    def dot(lhs, weights):
        return jnp.dot(lhs, weights, preferred_element_type=F32)

    def stacked(row, kind, j):
        return factors[row, kind, j].reshape(2 * max_rank, width)

    def outer(a, b):
        pair = jnp.concatenate(
            [
                jnp.concatenate([b[:max_rank], -b[max_rank:]], axis=0),
                jnp.concatenate([b[max_rank:], b[:max_rank]], axis=0),
            ],
            axis=1,
        )
        product = lax.dot_general(a, pair, (((0,), (0,)), ((), ())), preferred_element_type=F32).astype(BF16)
        return product[:, :width], product[:, width:]

    def make_dense(row, kind, g):
        first_kind, second_kind = (RIGHT, LEFT) if kind == UP else (LEFT, RIGHT)
        for j in range(g * size, (g + 1) * size):
            for part, x in enumerate(outer(stacked(row, first_kind, j), stacked(row, second_kind, j))):
                dense[row, kind, j, part] = x

    pltpu.make_async_copy(factors.at[core], factors.at[core], factor_sem).wait()
    load_rank.wait()
    for j in range(n):
        for part in range(2):
            for g in range(4):
                spot = pl.ds(g * step, step)
                piece = factors[core, LEFT, j, part, spot]
                factors[core, LEFT, j, part, spot] = jnp.where(
                    rank_ref[0, 0, j] > g, piece, jnp.zeros_like(piece)
                )
    give_left(0).start()
    for g in range(1, groups):
        give_right(g).start()
        give_left(g).start()
    for g in range(groups):
        make_dense(core, UP, g)
        make_dense(core, DOWN, g)

    load_layer.wait()
    square = (sources, sources)
    diagonal = lax.broadcasted_iota(jnp.int32, square, 0) == lax.broadcasted_iota(jnp.int32, square, 1)
    source_layer = jnp.sum(
        jnp.where(diagonal, jnp.broadcast_to(layer_ref[...], square), 0), axis=1, keepdims=True
    )
    source_layer = jnp.broadcast_to(source_layer, (sources, width))
    my_half = jnp.where(side == 0, source_layer[:half], source_layer[half:])
    my_half = jnp.concatenate([my_half, my_half], axis=0)
    pltpu.make_async_copy(own, own, load_sem.at[2]).wait()
    up_all[me] = jnp.where(side == 0, own[UP, :, :half], own[UP, :, half:])

    for g in range(groups):
        arrived(factors.at[1 - core, :, group(g)], twin_rsem.at[g])
        make_dense(1 - core, UP, g)
        if g < groups - 1:
            make_dense(1 - core, DOWN, g)

    def send_up(t):
        is_last = t == STEPS - 1

        @pl.when(has_above if is_last else feeds_up)
        def _():
            if is_last:
                for h in range(2):
                    up_last(h).start()
            else:
                for q in far_first:
                    up_step(t, q).start()

    def rise(t):
        is_last = t == STEPS - 1
        total = [up_base[h] if t > 0 else None for h in range(2)]
        for i, q in enumerate(chip_order if t == 0 else chip_order):
            if t == 0:
                pair = up_all.at[pl.ds(2 * q, 2)]
                arrived(up_all.at[twin] if i == 0 else pair, gather_rsem.at[q])
            else:
                pair = up_in.at[pl.ds((t - 1) * n + 2 * q, 2)]

                @pl.when(hears_up)
                def _():
                    arrived(pair, up_rsem.at[t - 1, q])

            lhs = spread([pair[h].reshape(rows, width) for h in range(2)])
            for h in range(2):
                term = dot(lhs, dense[h, UP, pl.ds(2 * q, 2)].reshape(4 * width, width))
                total[h] = term if total[h] is None else total[h] + term
        for h in range(2):
            if t == 0:
                total[h] = jnp.where(layer >= my_half, total[h], 0.0)
            if is_last:
                up_last_send[h] = total[h].astype(BF16)
            else:
                up_send[t, h] = total[h].astype(BF16)

        if t == 0:

            @pl.when(has_above)
            def _():
                pl.semaphore_wait(ready_sem, 1)

        if t == 0:
            for h in range(2):
                up_base[h] = total[h]
        send_up(t)

    def fall(t):
        is_last = t == STEPS - 1
        if t == 0:
            make_dense(1 - core, DOWN, groups - 1)

        if t == 0:

            @pl.when(has_above)
            def _():
                arrived(first_in, first_rsem)

        lhs = []
        blocks = [2 * q + h for q in far_first for h in range(2)]
        partial = {}
        for h in range(2):
            if t == 0:
                x = jnp.where(layer + 1 <= my_half, first_in[h].reshape(rows, width).astype(F32), 0.0)
            else:

                @pl.when(hears_down[t - 1])
                def _():
                    arrived(down_in.at[t - 1, :, h], down_rsem.at[t - 1, h])

                x = down_in[t - 1, 0, h].astype(F32)
                for q in range(1, chips):
                    x = x + down_in[t - 1, q, h].astype(F32)
            lhs.append(spread([x.astype(BF16)]))
            if t > 0 and h == 0:
                for i, j in enumerate(blocks):
                    partial[i] = down_base[j] + dot(lhs[0], dense[0, DOWN, j].reshape(2 * width, width))

        def back(i):
            j = blocks[i]
            if t == 0:
                out = dot(
                    jnp.concatenate(lhs, axis=1),
                    jnp.concatenate([dense[h, DOWN, j].reshape(2 * width, width) for h in range(2)], axis=0),
                )
                down_base[j] = out
                return out
            return partial[i] + dot(lhs[1], dense[1, DOWN, j].reshape(2 * width, width))

        if is_last:
            for i in range(n - 2):
                last_send[slot_of(blocks[i])] = back(i).astype(BF16)
            for i in range(n - 2):
                down_last(blocks[i]).start()
            near = [back(n - 2), back(n - 1)]
            last_send[slot_of(twin)] = jnp.where(core == 0, near[1], near[0]).astype(BF16)
            down_last(twin).start()
            mine[...] = jnp.where(core == 0, near[0], near[1])
            return
        for i in range(n):
            down_send[t * n + blocks[i]] = back(i).astype(BF16)

        @pl.when(feeds_down[t])
        def _():
            for h in range(2):
                for q in far_first:
                    down_step(t, q, h).start()

    for t in range(STEPS):
        rise(t)
        fall(t)

    def active(kind, keep):
        return [jnp.where(keep, own[kind, part].astype(F32), 0.0) for part in range(2)]

    def place(ref, start, halves):
        for h, x in enumerate(halves):
            for part in range(2):
                spot = pl.ds(h * half, half)
                ref[0, part, spot] = (
                    start[part][h * half:(h + 1) * half] + x[part * half:(part + 1) * half]
                ).astype(BF16)

    def finish_up():
        @pl.when(has_below)
        def _():
            arrived(up_in.at[pl.ds(inner, 2)], up_last_rsem)

        place(up_out, active_up, [up_in[inner + h].astype(F32) for h in range(2)])

    def finish_down():
        arrived(last_in, down_last_rsem)
        same, other = mine[...], 0.0
        for k in range(n - 1):
            x = last_in[k].astype(F32)
            if k % 2:
                same = same + x
            else:
                other = other + x
        place(
            down_out, active_down,
            [jnp.where(side == 0, same, other), jnp.where(side == 0, other, same)],
        )

    active_up = active(UP, layer >= source_layer)
    active_down = active(DOWN, layer <= source_layer)
    finish_up()
    finish_down()

    sent(factors.at[core], twin_ssem)
    sent(last, gather_ssem)

    def sent_when(condition, buffer, pieces, ssem):
        @pl.when(condition)
        def _():
            sent(buffer.at[pl.ds(0, pieces)], ssem)

    sent_when(feeds_up, up_in, inner + 2, up_ssem)
    sent_when(layer == layers - 2, up_in, 2, up_ssem)
    sent_when(feeds_down[0], down_send, inner + 2, down_ssem)
    sent_when(jnp.logical_and(layer == 1, has_above), down_send, inner + 2 - n, down_ssem)
    sent_when(jnp.logical_and(has_below, jnp.logical_not(has_above)), down_send, 2, down_ssem)


def hand_over(up_mem, down_mem, up_out, down_out, sems):
    stores = [
        pltpu.make_async_copy(mem, dst, sems.at[i])
        for i, (mem, dst) in enumerate([(up_mem, up_out), (down_mem, down_out)])
    ]
    for store in stores:
        store.start()
    for store in stores:
        store.wait()


def solution(mesh):
    layers, n = mesh.shape["gz"], mesh.shape["xy"]
    chips = n // 2

    def on_device(up_source, down_source, source_layer, u_factor, v_factor, block_rank):
        _, _, sources, width = up_source.shape
        half = sources // 2
        piece = (2 * half, width)
        anywhere = pl.BlockSpec(memory_space=pl.ANY)
        hbm = pl.BlockSpec(memory_space=pltpu.HBM)
        vmem = pl.BlockSpec(memory_space=pltpu.VMEM)
        dma = pltpu.SemaphoreType.DMA
        traces = pl.pallas_call(
            functools.partial(kernel, layers, n),
            out_shape=(pltpu.VMEM(up_source.shape, BF16), pltpu.VMEM(down_source.shape, BF16)),
            in_specs=[hbm] * 6,
            out_specs=(vmem, vmem),
            scratch_shapes=[
                pltpu.VMEM((1, sources), jnp.int32),
                pltpu.SMEM(block_rank.shape, jnp.int32),
                pltpu.VMEM((2, *up_source.shape[1:]), BF16),
                pltpu.VMEM((2, 2, *u_factor.shape[2:]), BF16),
                pltpu.VMEM((n, 2, half, width), BF16),
                pltpu.VMEM((2, 2, half, width), BF16),
                pltpu.VMEM((2, 2, n, 2, width, width), BF16),
                pltpu.VMEM((2, *piece), F32),
                pltpu.VMEM((n, *piece), F32),
                pltpu.VMEM(((STEPS - 1) * n + 2, *piece), BF16),
                pltpu.VMEM((STEPS - 1, 2, *piece), BF16),
                pltpu.VMEM((STEPS - 1, chips, 2, *piece), BF16),
                pltpu.VMEM(((STEPS - 1) * n + 2, *piece), BF16),
                pltpu.VMEM((2, *piece), BF16),
                pltpu.VMEM((2, n - 1, *piece), BF16),
                pltpu.VMEM(piece, F32),
                dma((3,)), dma,
                dma, dma((n,)),
                dma, dma((chips,)), dma,
                dma, dma((STEPS - 1, chips)), dma,
                dma, dma((STEPS - 1, 2)), dma,
                pltpu.SemaphoreType.REGULAR,
            ],
            compiler_params=pltpu.CompilerParams(collective_id=0, has_side_effects=True),
        )(up_source, down_source, source_layer.reshape(1, sources), u_factor, v_factor, block_rank)
        traces = [pltpu.with_memory_space_constraint(x, pltpu.VMEM) for x in traces]
        return pl.pallas_call(
            hand_over,
            out_shape=(
                jax.ShapeDtypeStruct(up_source.shape, BF16),
                jax.ShapeDtypeStruct(down_source.shape, BF16),
            ),
            in_specs=[vmem, vmem],
            out_specs=(anywhere, anywhere),
            scratch_shapes=[dma((2,))],
        )(*traces)

    in_specs = (
        P("gz", None, None, "xy"),
        P("gz", None, None, "xy"),
        P(),
        P("gz", "xy", None, None, None, None),
        P("gz", "xy", None, None, None, None),
        P("gz", "xy", None),
    )
    out_specs = (P("gz", None, None, "xy"), P("gz", None, None, "xy"))
    return jax.shard_map(
        on_device, mesh=mesh, in_specs=in_specs, out_specs=out_specs, check_vma=False
    )
```

```python
import functools

import jax
import jax.numpy as jnp
from jax import lax
from jax.experimental import pallas as pl
from jax.experimental.pallas import tpu as pltpu
from jax.sharding import PartitionSpec as P

STEPS = 3
MESH = pl.DeviceIdType.MESH
F32, BF16 = jnp.float32, jnp.bfloat16
UP, DOWN = 0, 1
LEFT, RIGHT = 0, 1


def kernel(
    layers, n, up_hbm, down_hbm, layer_hbm, u_hbm, v_hbm, rank_hbm, up_out, down_out,
    layer_ref, rank_ref, own, factors, up_all, first_in, dense, up_base, down_base,
    up_in, up_send, down_in, down_send, up_last_send, last, mine,
    load_sem, factor_sem, twin_ssem, twin_rsem, gather_ssem, gather_rsem, first_rsem,
    up_ssem, up_rsem, up_last_rsem, down_ssem, down_rsem, down_last_rsem, ready_sem,
):
    layer = lax.axis_index("gz")
    me = lax.axis_index("xy")
    has_above = layer < layers - 1
    has_below = layer > 0
    chips = n // 2
    chip = me // 2
    core = lax.rem(me, 2)
    side = lax.rem(core + layer, 2)
    twin = me + 1 - 2 * core
    _, _, sources, width = own.shape
    half = sources // 2
    rows = 2 * half
    max_rank = factors.shape[4]
    step = max_rank // 4
    chip_order = [lax.rem(chip + k, chips) for k in range(chips)]
    far_chips = chip_order[1:]
    far_first = [*far_chips, chip]
    inner = (STEPS - 1) * n
    last_in, last_send = last.at[0], last.at[1]

    def remote(src, dst, ssem, rsem, to_layer, to_block):
        return pltpu.make_async_remote_copy(
            src_ref=src, dst_ref=dst, send_sem=ssem, recv_sem=rsem,
            device_id={"gz": to_layer, "xy": to_block}, device_id_type=MESH,
        )

    def arrived(ref, rsem):
        remote(ref, ref, gather_ssem, rsem, layer, me).wait_recv()

    def sent(ref, ssem):
        remote(ref, ref, ssem, twin_rsem.at[0], layer, me).wait_send()

    def tell(sem, to_layer, to_block):
        pl.semaphore_signal(
            sem, inc=1, device_id={"gz": to_layer, "xy": to_block}, device_id_type=MESH
        )

    barrier = pltpu.get_barrier_semaphore()

    @pl.when(has_above)
    def _():
        tell(barrier, layer + 1, me)
        tell(barrier, layer + 1, twin)

    for q in far_chips:
        for h in range(2):
            tell(barrier, layer, 2 * q + h)
    tell(barrier, layer, twin)

    def half_of(ref, h):
        return ref.at[0, :, pl.ds(pl.multiple_of(h * half, half), half)]

    load_factors = [
        pltpu.make_async_copy(hbm.at[0, 0], factors.at[core, kind], factor_sem)
        for kind, hbm in ((LEFT, u_hbm), (RIGHT, v_hbm))
    ]
    load_rank = pltpu.make_async_copy(rank_hbm, rank_ref, load_sem.at[0])
    load_layer = pltpu.make_async_copy(layer_hbm, layer_ref, load_sem.at[1])
    load_own = [
        pltpu.make_async_copy(hbm.at[0], own.at[kind], load_sem.at[2]) for kind, hbm in ((UP, up_hbm), (DOWN, down_hbm))
    ]
    for load in (*load_factors, load_rank, load_layer, *load_own):
        load.start()

    hears_up = jnp.logical_and(has_below, has_above)
    feeds_up = layer < layers - 2
    hears_down = [jnp.logical_and(has_below, feeds_up), feeds_up]
    feeds_down = [jnp.logical_and(layer > 1, has_above), jnp.logical_and(has_below, has_above)]

    @pl.when(jnp.logical_not(hears_up))
    def _():
        up_in[:inner] = jnp.zeros_like(up_in[:inner])

    @pl.when(jnp.logical_not(has_below))
    def _():
        up_in[inner:] = jnp.zeros_like(up_in[inner:])

    @pl.when(jnp.logical_not(has_above))
    def _():
        first_in[...] = jnp.zeros_like(first_in)

    for t in range(STEPS - 1):

        @pl.when(jnp.logical_not(hears_down[t]))
        def _():
            down_in[t] = jnp.zeros_like(down_in[t])

    pl.semaphore_wait(barrier, n - 1 + jnp.where(has_below, 2, 0))

    def gather(to, h):
        return remote(half_of(up_hbm, h), up_all.at[me], gather_ssem, gather_rsem.at[chip], layer, to)

    def first(h):
        return remote(
            half_of(down_hbm, lax.rem(layer + 1 + h, 2)), first_in.at[core], down_ssem, first_rsem, layer - 1, 2 * chip + h
        )

    groups = n
    size = n // groups

    def group(g):
        return pl.ds(g * size, size)

    def give_left(g):
        slot = factors.at[core, LEFT, group(g)]
        return remote(slot, slot, twin_ssem, twin_rsem.at[g], layer, twin)

    def give_right(g):
        return remote(
            v_hbm.at[0, 0, group(g)], factors.at[core, RIGHT, group(g)], twin_ssem, twin_rsem.at[g], layer, twin
        )

    def up_step(t, q):
        return remote(
            up_send.at[t], up_in.at[pl.ds(t * n + 2 * chip, 2)], up_ssem, up_rsem.at[t, chip], layer + 1, 2 * q + 1 - core
        )

    def up_last(h):
        return remote(
            up_last_send.at[h], up_in.at[inner + side], up_ssem, up_last_rsem, layer + 1, 2 * chip + h
        )

    def down_step(t, q, h):
        return remote(
            down_send.at[t * n + 2 * q + h], down_in.at[t, chip, h], down_ssem, down_rsem.at[t, h],
            layer - 1, 2 * q + 1 - core,
        )

    def slot_of(to):
        return lax.rem(to - me + n, n) - 1

    def down_last(to):
        slot = slot_of(to)
        return remote(
            last_send.at[slot], last_in.at[n - 2 - slot], gather_ssem, down_last_rsem, layer, to
        )

    for q in far_chips:
        for h in range(2):
            gather(2 * q + h, lax.rem(layer + h, 2)).start()

    @pl.when(has_below)
    def _():
        for h in range(2):
            first(h).start()
        tell(ready_sem, layer - 1, me)

    gather(twin, 1 - side).start()
    give_right(0).start()

    def turned(x):
        middle = x.shape[0] // 2
        return jnp.concatenate([-x[middle:], x[:middle]], axis=0)

    def spread(blocks):
        return jnp.concatenate([side for x in blocks for side in (x, turned(x))], axis=1)

    def dot(lhs, weights):
        return jnp.dot(lhs, weights, preferred_element_type=F32)

    def stacked(row, kind, j):
        return factors[row, kind, j].reshape(2 * max_rank, width)

    def outer(a, b):
        pair = jnp.concatenate(
            [
                jnp.concatenate([b[:max_rank], -b[max_rank:]], axis=0),
                jnp.concatenate([b[max_rank:], b[:max_rank]], axis=0),
            ],
            axis=1,
        )
        product = lax.dot_general(a, pair, (((0,), (0,)), ((), ())), preferred_element_type=F32).astype(BF16)
        return product[:, :width], product[:, width:]

    def make_dense(row, kind, g):
        first_kind, second_kind = (RIGHT, LEFT) if kind == UP else (LEFT, RIGHT)
        for j in range(g * size, (g + 1) * size):
            for part, x in enumerate(outer(stacked(row, first_kind, j), stacked(row, second_kind, j))):
                dense[row, kind, j, part] = x

    pltpu.make_async_copy(factors.at[core], factors.at[core], factor_sem).wait()
    load_rank.wait()
    for j in range(n):
        for part in range(2):
            for g in range(4):
                spot = pl.ds(g * step, step)
                piece = factors[core, LEFT, j, part, spot]
                factors[core, LEFT, j, part, spot] = jnp.where(
                    rank_ref[0, 0, j] > g, piece, jnp.zeros_like(piece)
                )
    give_left(0).start()
    for g in range(1, groups):
        give_right(g).start()
        give_left(g).start()
    for g in range(groups):
        make_dense(core, UP, g)
        make_dense(core, DOWN, g)

    load_layer.wait()
    square = (sources, sources)
    diagonal = lax.broadcasted_iota(jnp.int32, square, 0) == lax.broadcasted_iota(jnp.int32, square, 1)
    source_layer = jnp.sum(
        jnp.where(diagonal, jnp.broadcast_to(layer_ref[...], square), 0), axis=1, keepdims=True
    )
    source_layer = jnp.broadcast_to(source_layer, (sources, width))
    my_half = jnp.where(side == 0, source_layer[:half], source_layer[half:])
    my_half = jnp.concatenate([my_half, my_half], axis=0)
    pltpu.make_async_copy(own, own, load_sem.at[2]).wait()
    up_all[me] = jnp.where(side == 0, own[UP, :, :half], own[UP, :, half:])

    for g in range(groups):
        arrived(factors.at[1 - core, :, group(g)], twin_rsem.at[g])
        make_dense(1 - core, UP, g)
        if g < groups - 1:
            make_dense(1 - core, DOWN, g)

    def send_up(t):
        is_last = t == STEPS - 1

        @pl.when(has_above if is_last else feeds_up)
        def _():
            if is_last:
                for h in range(2):
                    up_last(h).start()
            else:
                for q in [jnp.where(core == 0, a, b) for a, b in zip(far_first, chip_order)]:
                    up_step(t, q).start()

    def rise(t):
        is_last = t == STEPS - 1
        total = [up_base[h] if t > 0 else None for h in range(2)]
        for i, q in enumerate(chip_order if t == 0 else chip_order):
            if t == 0:
                pair = up_all.at[pl.ds(2 * q, 2)]
                arrived(up_all.at[twin] if i == 0 else pair, gather_rsem.at[q])
            else:
                pair = up_in.at[pl.ds((t - 1) * n + 2 * q, 2)]

                @pl.when(hears_up)
                def _():
                    arrived(pair, up_rsem.at[t - 1, q])

            lhs = spread([pair[h].reshape(rows, width) for h in range(2)])
            for h in range(2):
                term = dot(lhs, dense[h, UP, pl.ds(2 * q, 2)].reshape(4 * width, width))
                total[h] = term if total[h] is None else total[h] + term
        for h in range(2):
            if t == 0:
                total[h] = jnp.where(layer >= my_half, total[h], 0.0)
            if is_last:
                up_last_send[h] = total[h].astype(BF16)
            else:
                up_send[t, h] = total[h].astype(BF16)

        if t == 0:

            @pl.when(has_above)
            def _():
                pl.semaphore_wait(ready_sem, 1)

        send_up(t)
        if t == 0:
            for h in range(2):
                up_base[h] = total[h]

    def fall(t):
        is_last = t == STEPS - 1
        if t == 0:
            make_dense(1 - core, DOWN, groups - 1)

        if t == 0:

            @pl.when(has_above)
            def _():
                arrived(first_in, first_rsem)

        lhs = []
        blocks = [2 * q + h for q in far_first for h in range(2)]
        partial = {}
        for h in range(2):
            if t == 0:
                x = jnp.where(layer + 1 <= my_half, first_in[h].reshape(rows, width).astype(F32), 0.0)
            else:

                @pl.when(hears_down[t - 1])
                def _():
                    arrived(down_in.at[t - 1, :, h], down_rsem.at[t - 1, h])

                x = down_in[t - 1, 0, h].astype(F32)
                for q in range(1, chips):
                    x = x + down_in[t - 1, q, h].astype(F32)
            lhs.append(spread([x.astype(BF16)]))
            if t > 0 and h == 0:
                for i, j in enumerate(blocks[:n - 2] if is_last else blocks):
                    partial[i] = down_base[j] + dot(lhs[0], dense[0, DOWN, j].reshape(2 * width, width))

        def back(i):
            j = blocks[i]
            if i not in partial:
                out = dot(
                    jnp.concatenate(lhs, axis=1),
                    jnp.concatenate([dense[h, DOWN, j].reshape(2 * width, width) for h in range(2)], axis=0),
                )
                if t > 0:
                    return down_base[j] + out
                down_base[j] = out
                return out
            return partial[i] + dot(lhs[1], dense[1, DOWN, j].reshape(2 * width, width))

        if is_last:
            for i in range(n - 2):
                last_send[slot_of(blocks[i])] = back(i).astype(BF16)
            for i in range(n - 2):
                down_last(blocks[i]).start()
            near = [back(n - 2), back(n - 1)]
            last_send[slot_of(twin)] = jnp.where(core == 0, near[1], near[0]).astype(BF16)
            down_last(twin).start()
            mine[...] = jnp.where(core == 0, near[0], near[1])
            return
        for i in range(n):
            down_send[t * n + blocks[i]] = back(i).astype(BF16)

        @pl.when(feeds_down[t])
        def _():
            for h in range(2):
                for q in far_first:
                    down_step(t, q, h).start()

    for t in range(STEPS):
        rise(t)
        fall(t)

    def active(kind, keep):
        return [jnp.where(keep, own[kind, part].astype(F32), 0.0) for part in range(2)]

    def place(ref, start, halves):
        for h, x in enumerate(halves):
            for part in range(2):
                spot = pl.ds(h * half, half)
                ref[0, part, spot] = (
                    start[part][h * half:(h + 1) * half] + x[part * half:(part + 1) * half]
                ).astype(BF16)

    def finish_up():
        @pl.when(has_below)
        def _():
            arrived(up_in.at[pl.ds(inner, 2)], up_last_rsem)

        place(up_out, active_up, [up_in[inner + h].astype(F32) for h in range(2)])

    def finish_down():
        arrived(last_in, down_last_rsem)
        same, other = mine[...], 0.0
        for k in range(n - 1):
            x = last_in[k].astype(F32)
            if k % 2:
                same = same + x
            else:
                other = other + x
        place(
            down_out, active_down,
            [jnp.where(side == 0, same, other), jnp.where(side == 0, other, same)],
        )

    active_up = active(UP, layer >= source_layer)
    active_down = active(DOWN, layer <= source_layer)
    finish_up()
    finish_down()

    sent(factors.at[core], twin_ssem)
    sent(last, gather_ssem)

    def sent_when(condition, buffer, pieces, ssem):
        @pl.when(condition)
        def _():
            sent(buffer.at[pl.ds(0, pieces)], ssem)

    sent_when(feeds_up, up_in, inner + 2, up_ssem)
    sent_when(layer == layers - 2, up_in, 2, up_ssem)
    sent_when(feeds_down[0], down_send, inner + 2, down_ssem)
    sent_when(jnp.logical_and(layer == 1, has_above), down_send, inner + 2 - n, down_ssem)
    sent_when(jnp.logical_and(has_below, jnp.logical_not(has_above)), down_send, 2, down_ssem)


def hand_over(up_mem, down_mem, up_out, down_out, sems):
    stores = [
        pltpu.make_async_copy(mem, dst, sems.at[i])
        for i, (mem, dst) in enumerate([(up_mem, up_out), (down_mem, down_out)])
    ]
    for store in stores:
        store.start()
    for store in stores:
        store.wait()


def solution(mesh):
    layers, n = mesh.shape["gz"], mesh.shape["xy"]
    chips = n // 2

    def on_device(up_source, down_source, source_layer, u_factor, v_factor, block_rank):
        _, _, sources, width = up_source.shape
        half = sources // 2
        piece = (2 * half, width)
        anywhere = pl.BlockSpec(memory_space=pl.ANY)
        hbm = pl.BlockSpec(memory_space=pltpu.HBM)
        vmem = pl.BlockSpec(memory_space=pltpu.VMEM)
        dma = pltpu.SemaphoreType.DMA
        traces = pl.pallas_call(
            functools.partial(kernel, layers, n),
            out_shape=(pltpu.VMEM(up_source.shape, BF16), pltpu.VMEM(down_source.shape, BF16)),
            in_specs=[hbm] * 6,
            out_specs=(vmem, vmem),
            scratch_shapes=[
                pltpu.VMEM((1, sources), jnp.int32),
                pltpu.SMEM(block_rank.shape, jnp.int32),
                pltpu.VMEM((2, *up_source.shape[1:]), BF16),
                pltpu.VMEM((2, 2, *u_factor.shape[2:]), BF16),
                pltpu.VMEM((n, 2, half, width), BF16),
                pltpu.VMEM((2, 2, half, width), BF16),
                pltpu.VMEM((2, 2, n, 2, width, width), BF16),
                pltpu.VMEM((2, *piece), F32),
                pltpu.VMEM((n, *piece), F32),
                pltpu.VMEM(((STEPS - 1) * n + 2, *piece), BF16),
                pltpu.VMEM((STEPS - 1, 2, *piece), BF16),
                pltpu.VMEM((STEPS - 1, chips, 2, *piece), BF16),
                pltpu.VMEM(((STEPS - 1) * n + 2, *piece), BF16),
                pltpu.VMEM((2, *piece), BF16),
                pltpu.VMEM((2, n - 1, *piece), BF16),
                pltpu.VMEM(piece, F32),
                dma((3,)), dma,
                dma, dma((n,)),
                dma, dma((chips,)), dma,
                dma, dma((STEPS - 1, chips)), dma,
                dma, dma((STEPS - 1, 2)), dma,
                pltpu.SemaphoreType.REGULAR,
            ],
            compiler_params=pltpu.CompilerParams(collective_id=0, has_side_effects=True),
        )(up_source, down_source, source_layer.reshape(1, sources), u_factor, v_factor, block_rank)
        traces = [pltpu.with_memory_space_constraint(x, pltpu.VMEM) for x in traces]
        return pl.pallas_call(
            hand_over,
            out_shape=(
                jax.ShapeDtypeStruct(up_source.shape, BF16),
                jax.ShapeDtypeStruct(down_source.shape, BF16),
            ),
            in_specs=[vmem, vmem],
            out_specs=(anywhere, anywhere),
            scratch_shapes=[dma((2,))],
        )(*traces)

    in_specs = (
        P("gz", None, None, "xy"),
        P("gz", None, None, "xy"),
        P(),
        P("gz", "xy", None, None, None, None),
        P("gz", "xy", None, None, None, None),
        P("gz", "xy", None),
    )
    out_specs = (P("gz", None, None, "xy"), P("gz", None, None, "xy"))
    return jax.shard_map(
        on_device, mesh=mesh, in_specs=in_specs, out_specs=out_specs, check_vma=False
    )
```

```python
import functools

import jax
import jax.numpy as jnp
from jax import lax
from jax.experimental import pallas as pl
from jax.experimental.pallas import tpu as pltpu
from jax.sharding import PartitionSpec as P

STEPS = 3
MESH = pl.DeviceIdType.MESH
F32, BF16 = jnp.float32, jnp.bfloat16
UP, DOWN = 0, 1
LEFT, RIGHT = 0, 1


def kernel(
    layers, n, up_hbm, down_hbm, layer_hbm, u_hbm, v_hbm, rank_hbm, up_out, down_out,
    layer_ref, rank_ref, own, factors, up_all, first_in, dense, up_base, down_base,
    up_in, up_send, down_in, down_send, up_last_send, last, mine,
    load_sem, factor_sem, twin_ssem, twin_rsem, gather_ssem, gather_rsem, first_rsem,
    up_ssem, up_rsem, up_last_rsem, down_ssem, down_rsem, down_last_rsem, ready_sem,
):
    layer = lax.axis_index("gz")
    me = lax.axis_index("xy")
    has_above = layer < layers - 1
    has_below = layer > 0
    chips = n // 2
    chip = me // 2
    core = lax.rem(me, 2)
    side = lax.rem(core + layer, 2)
    twin = me + 1 - 2 * core
    _, _, sources, width = own.shape
    half = sources // 2
    rows = 2 * half
    max_rank = factors.shape[4]
    step = max_rank // 4
    chip_order = [lax.rem(chip + k, chips) for k in range(chips)]
    far_chips = chip_order[1:]
    far_first = [*far_chips, chip]
    inner = (STEPS - 1) * n
    last_in, last_send = last.at[0], last.at[1]

    def remote(src, dst, ssem, rsem, to_layer, to_block):
        return pltpu.make_async_remote_copy(
            src_ref=src, dst_ref=dst, send_sem=ssem, recv_sem=rsem,
            device_id={"gz": to_layer, "xy": to_block}, device_id_type=MESH,
        )

    def arrived(ref, rsem):
        remote(ref, ref, gather_ssem, rsem, layer, me).wait_recv()

    def sent(ref, ssem):
        remote(ref, ref, ssem, twin_rsem.at[0], layer, me).wait_send()

    def tell(sem, to_layer, to_block):
        pl.semaphore_signal(
            sem, inc=1, device_id={"gz": to_layer, "xy": to_block}, device_id_type=MESH
        )

    barrier = pltpu.get_barrier_semaphore()

    @pl.when(has_above)
    def _():
        tell(barrier, layer + 1, me)
        tell(barrier, layer + 1, twin)

    for q in far_chips:
        for h in range(2):
            tell(barrier, layer, 2 * q + h)
    tell(barrier, layer, twin)

    def half_of(ref, h):
        return ref.at[0, :, pl.ds(pl.multiple_of(h * half, half), half)]

    load_factors = [
        pltpu.make_async_copy(hbm.at[0, 0], factors.at[core, kind], factor_sem)
        for kind, hbm in ((LEFT, u_hbm), (RIGHT, v_hbm))
    ]
    load_rank = pltpu.make_async_copy(rank_hbm, rank_ref, load_sem.at[0])
    load_layer = pltpu.make_async_copy(layer_hbm, layer_ref, load_sem.at[1])
    load_own = [
        pltpu.make_async_copy(hbm.at[0], own.at[kind], load_sem.at[2]) for kind, hbm in ((UP, up_hbm), (DOWN, down_hbm))
    ]
    for load in (*load_factors, load_rank, load_layer, *load_own):
        load.start()

    feeds_up = [layer < layers - STEPS + t for t in range(STEPS)]
    hears_up = [jnp.logical_and(has_below, layer - 1 < layers - STEPS + t) for t in range(STEPS - 1)]
    low = layer < layers - 2
    hears_down = [jnp.logical_and(has_below, low), low]
    feeds_down = [jnp.logical_and(layer > 1, has_above), jnp.logical_and(has_below, has_above)]

    for t in range(STEPS - 1):

        @pl.when(jnp.logical_not(hears_up[t]))
        def _():
            up_in[t * n:(t + 1) * n] = jnp.zeros_like(up_in[t * n:(t + 1) * n])

    @pl.when(jnp.logical_not(has_below))
    def _():
        up_in[inner:] = jnp.zeros_like(up_in[inner:])

    @pl.when(jnp.logical_not(has_above))
    def _():
        first_in[...] = jnp.zeros_like(first_in)

    for t in range(STEPS - 1):

        @pl.when(jnp.logical_not(hears_down[t]))
        def _():
            down_in[t] = jnp.zeros_like(down_in[t])

    pl.semaphore_wait(barrier, n - 1 + jnp.where(has_below, 2, 0))

    def gather(to, h):
        return remote(half_of(up_hbm, h), up_all.at[me], gather_ssem, gather_rsem.at[chip], layer, to)

    def first(h):
        return remote(
            half_of(down_hbm, lax.rem(layer + 1 + h, 2)), first_in.at[core], down_ssem, first_rsem, layer - 1, 2 * chip + h
        )

    groups = n
    size = n // groups

    def group(g):
        return pl.ds(g * size, size)

    def give_left(g):
        slot = factors.at[core, LEFT, group(g)]
        return remote(slot, slot, twin_ssem, twin_rsem.at[g], layer, twin)

    def give_right(g):
        return remote(
            v_hbm.at[0, 0, group(g)], factors.at[core, RIGHT, group(g)], twin_ssem, twin_rsem.at[g], layer, twin
        )

    def up_step(t, q):
        return remote(
            up_send.at[t], up_in.at[pl.ds(t * n + 2 * chip, 2)], up_ssem, up_rsem.at[t, chip], layer + 1, 2 * q + 1 - core
        )

    def up_last(h):
        return remote(
            up_last_send.at[h], up_in.at[inner + side], up_ssem, up_last_rsem, layer + 1, 2 * chip + h
        )

    def down_step(t, q, h):
        return remote(
            down_send.at[t * n + 2 * q + h], down_in.at[t, chip, h], down_ssem, down_rsem.at[t, h],
            layer - 1, 2 * q + 1 - core,
        )

    def slot_of(to):
        return lax.rem(to - me + n, n) - 1

    def down_last(to):
        slot = slot_of(to)
        return remote(
            last_send.at[slot], last_in.at[n - 2 - slot], gather_ssem, down_last_rsem, layer, to
        )

    for q in far_chips:
        for h in range(2):
            gather(2 * q + h, lax.rem(layer + h, 2)).start()

    @pl.when(has_below)
    def _():
        for h in range(2):
            first(h).start()
        tell(ready_sem, layer - 1, me)

    gather(twin, 1 - side).start()
    give_right(0).start()

    def turned(x):
        middle = x.shape[0] // 2
        return jnp.concatenate([-x[middle:], x[:middle]], axis=0)

    def spread(blocks):
        return jnp.concatenate([side for x in blocks for side in (x, turned(x))], axis=1)

    def dot(lhs, weights):
        return jnp.dot(lhs, weights, preferred_element_type=F32)

    def stacked(row, kind, j):
        return factors[row, kind, j].reshape(2 * max_rank, width)

    def outer(a, b):
        pair = jnp.concatenate(
            [
                jnp.concatenate([b[:max_rank], -b[max_rank:]], axis=0),
                jnp.concatenate([b[max_rank:], b[:max_rank]], axis=0),
            ],
            axis=1,
        )
        product = lax.dot_general(a, pair, (((0,), (0,)), ((), ())), preferred_element_type=F32).astype(BF16)
        return product[:, :width], product[:, width:]

    def make_dense(row, kind, g):
        first_kind, second_kind = (RIGHT, LEFT) if kind == UP else (LEFT, RIGHT)
        for j in range(g * size, (g + 1) * size):
            for part, x in enumerate(outer(stacked(row, first_kind, j), stacked(row, second_kind, j))):
                dense[row, kind, j, part] = x

    pltpu.make_async_copy(factors.at[core], factors.at[core], factor_sem).wait()
    load_rank.wait()
    for j in range(n):
        for part in range(2):
            for g in range(4):
                spot = pl.ds(g * step, step)
                piece = factors[core, LEFT, j, part, spot]
                factors[core, LEFT, j, part, spot] = jnp.where(
                    rank_ref[0, 0, j] > g, piece, jnp.zeros_like(piece)
                )
    give_left(0).start()
    for g in range(1, groups):
        give_right(g).start()
        give_left(g).start()
    for g in range(groups):
        make_dense(core, UP, g)
        make_dense(core, DOWN, g)

    load_layer.wait()
    square = (sources, sources)
    diagonal = lax.broadcasted_iota(jnp.int32, square, 0) == lax.broadcasted_iota(jnp.int32, square, 1)
    source_layer = jnp.sum(
        jnp.where(diagonal, jnp.broadcast_to(layer_ref[...], square), 0), axis=1, keepdims=True
    )
    source_layer = jnp.broadcast_to(source_layer, (sources, width))
    my_half = jnp.where(side == 0, source_layer[:half], source_layer[half:])
    my_half = jnp.concatenate([my_half, my_half], axis=0)
    pltpu.make_async_copy(own, own, load_sem.at[2]).wait()
    up_all[me] = jnp.where(side == 0, own[UP, :, :half], own[UP, :, half:])

    for g in range(groups):
        arrived(factors.at[1 - core, :, group(g)], twin_rsem.at[g])
        make_dense(1 - core, UP, g)
        if g < groups - 1:
            make_dense(1 - core, DOWN, g)

    def send_up(t):
        is_last = t == STEPS - 1

        @pl.when(feeds_up[t])
        def _():
            if is_last:
                for h in range(2):
                    up_last(h).start()
            else:
                for q in far_first:
                    up_step(t, q).start()

    def rise(t):
        is_last = t == STEPS - 1
        total = [up_base[h] if t > 0 else None for h in range(2)]
        for i, q in enumerate(chip_order if t == 0 else chip_order):
            if t == 0:
                pair = up_all.at[pl.ds(2 * q, 2)]
                arrived(up_all.at[twin] if i == 0 else pair, gather_rsem.at[q])
            else:
                pair = up_in.at[pl.ds((t - 1) * n + 2 * q, 2)]

                @pl.when(hears_up[t - 1])
                def _():
                    arrived(pair, up_rsem.at[t - 1, q])

            lhs = spread([pair[h].reshape(rows, width) for h in range(2)])
            for h in range(2):
                term = dot(lhs, dense[h, UP, pl.ds(2 * q, 2)].reshape(4 * width, width))
                total[h] = term if total[h] is None else total[h] + term
        for h in range(2):
            if t == 0:
                total[h] = jnp.where(layer >= my_half, total[h], 0.0)
            if is_last:
                up_last_send[h] = total[h].astype(BF16)
            else:
                up_send[t, h] = total[h].astype(BF16)

        if t == 0:

            @pl.when(has_above)
            def _():
                pl.semaphore_wait(ready_sem, 1)

        send_up(t)
        if t == 0:
            for h in range(2):
                up_base[h] = total[h]

    def fall(t):
        is_last = t == STEPS - 1
        if t == 0:
            make_dense(1 - core, DOWN, groups - 1)

        if t == 0:

            @pl.when(has_above)
            def _():
                arrived(first_in, first_rsem)

        lhs = []
        blocks = [2 * q + h for q in far_first for h in range(2)]
        partial, fresh = {}, {}
        for h in range(2):
            if t == 0:
                x = jnp.where(layer + 1 <= my_half, first_in[h].reshape(rows, width).astype(F32), 0.0)
            else:

                @pl.when(hears_down[t - 1])
                def _():
                    arrived(down_in.at[t - 1, :, h], down_rsem.at[t - 1, h])

                x = down_in[t - 1, 0, h].astype(F32)
                for q in range(1, chips):
                    x = x + down_in[t - 1, q, h].astype(F32)
            lhs.append(spread([x.astype(BF16)]))
            if t > 0 and h == 0:
                for i, j in enumerate(blocks[:n - 2] if is_last else blocks):
                    partial[i] = down_base[j] + dot(lhs[0], dense[0, DOWN, j].reshape(2 * width, width))

        def back(i):
            j = blocks[i]
            if i not in partial:
                out = dot(
                    jnp.concatenate(lhs, axis=1),
                    jnp.concatenate([dense[h, DOWN, j].reshape(2 * width, width) for h in range(2)], axis=0),
                )
                if t > 0:
                    return down_base[j] + out
                fresh[i] = out
                return out
            return partial[i] + dot(lhs[1], dense[1, DOWN, j].reshape(2 * width, width))

        if is_last:
            for i in range(n - 2):
                last_send[slot_of(blocks[i])] = back(i).astype(BF16)
            for i in range(n - 2):
                down_last(blocks[i]).start()
            near = [back(n - 2), back(n - 1)]
            last_send[slot_of(twin)] = jnp.where(core == 0, near[1], near[0]).astype(BF16)
            down_last(twin).start()
            mine[...] = jnp.where(core == 0, near[0], near[1])
            return
        for i in range(n):
            down_send[t * n + blocks[i]] = back(i).astype(BF16)

        @pl.when(feeds_down[t])
        def _():
            for h in range(2):
                for q in far_first:
                    down_step(t, q, h).start()

        for i, out in fresh.items():
            down_base[blocks[i]] = out

    for t in range(STEPS):
        rise(t)
        fall(t)

    def active(kind, keep):
        return [jnp.where(keep, own[kind, part].astype(F32), 0.0) for part in range(2)]

    def place(ref, start, halves):
        for h, x in enumerate(halves):
            for part in range(2):
                spot = pl.ds(h * half, half)
                ref[0, part, spot] = (
                    start[part][h * half:(h + 1) * half] + x[part * half:(part + 1) * half]
                ).astype(BF16)

    def finish_up():
        @pl.when(has_below)
        def _():
            arrived(up_in.at[pl.ds(inner, 2)], up_last_rsem)

        place(up_out, active_up, [up_in[inner + h].astype(F32) for h in range(2)])

    def finish_down():
        arrived(last_in, down_last_rsem)
        same, other = mine[...], 0.0
        for k in range(n - 1):
            x = last_in[k].astype(F32)
            if k % 2:
                same = same + x
            else:
                other = other + x
        place(
            down_out, active_down,
            [jnp.where(side == 0, same, other), jnp.where(side == 0, other, same)],
        )

    active_up = active(UP, layer >= source_layer)
    active_down = active(DOWN, layer <= source_layer)
    finish_up()
    finish_down()

    sent(factors.at[core], twin_ssem)
    sent(last, gather_ssem)

    def sent_when(condition, buffer, pieces, ssem):
        @pl.when(condition)
        def _():
            sent(buffer.at[pl.ds(0, pieces)], ssem)

    for t in range(STEPS):
        began = feeds_up[0] if t == 0 else jnp.logical_and(feeds_up[t], jnp.logical_not(feeds_up[t - 1]))
        sent_when(began, up_in, inner + 2 - t * n, up_ssem)
    sent_when(feeds_down[0], down_send, inner + 2, down_ssem)
    sent_when(jnp.logical_and(layer == 1, has_above), down_send, inner + 2 - n, down_ssem)
    sent_when(jnp.logical_and(has_below, jnp.logical_not(has_above)), down_send, 2, down_ssem)


def hand_over(up_mem, down_mem, up_out, down_out, sems):
    stores = [
        pltpu.make_async_copy(mem, dst, sems.at[i])
        for i, (mem, dst) in enumerate([(up_mem, up_out), (down_mem, down_out)])
    ]
    for store in stores:
        store.start()
    for store in stores:
        store.wait()


def solution(mesh):
    layers, n = mesh.shape["gz"], mesh.shape["xy"]
    chips = n // 2

    def on_device(up_source, down_source, source_layer, u_factor, v_factor, block_rank):
        _, _, sources, width = up_source.shape
        half = sources // 2
        piece = (2 * half, width)
        anywhere = pl.BlockSpec(memory_space=pl.ANY)
        hbm = pl.BlockSpec(memory_space=pltpu.HBM)
        vmem = pl.BlockSpec(memory_space=pltpu.VMEM)
        dma = pltpu.SemaphoreType.DMA
        traces = pl.pallas_call(
            functools.partial(kernel, layers, n),
            out_shape=(pltpu.VMEM(up_source.shape, BF16), pltpu.VMEM(down_source.shape, BF16)),
            in_specs=[hbm] * 6,
            out_specs=(vmem, vmem),
            scratch_shapes=[
                pltpu.VMEM((1, sources), jnp.int32),
                pltpu.SMEM(block_rank.shape, jnp.int32),
                pltpu.VMEM((2, *up_source.shape[1:]), BF16),
                pltpu.VMEM((2, 2, *u_factor.shape[2:]), BF16),
                pltpu.VMEM((n, 2, half, width), BF16),
                pltpu.VMEM((2, 2, half, width), BF16),
                pltpu.VMEM((2, 2, n, 2, width, width), BF16),
                pltpu.VMEM((2, *piece), F32),
                pltpu.VMEM((n, *piece), F32),
                pltpu.VMEM(((STEPS - 1) * n + 2, *piece), BF16),
                pltpu.VMEM((STEPS - 1, 2, *piece), BF16),
                pltpu.VMEM((STEPS - 1, chips, 2, *piece), BF16),
                pltpu.VMEM(((STEPS - 1) * n + 2, *piece), BF16),
                pltpu.VMEM((2, *piece), BF16),
                pltpu.VMEM((2, n - 1, *piece), BF16),
                pltpu.VMEM(piece, F32),
                dma((3,)), dma,
                dma, dma((n,)),
                dma, dma((chips,)), dma,
                dma, dma((STEPS - 1, chips)), dma,
                dma, dma((STEPS - 1, 2)), dma,
                pltpu.SemaphoreType.REGULAR,
            ],
            compiler_params=pltpu.CompilerParams(collective_id=0, has_side_effects=True),
        )(up_source, down_source, source_layer.reshape(1, sources), u_factor, v_factor, block_rank)
        traces = [pltpu.with_memory_space_constraint(x, pltpu.VMEM) for x in traces]
        return pl.pallas_call(
            hand_over,
            out_shape=(
                jax.ShapeDtypeStruct(up_source.shape, BF16),
                jax.ShapeDtypeStruct(down_source.shape, BF16),
            ),
            in_specs=[vmem, vmem],
            out_specs=(anywhere, anywhere),
            scratch_shapes=[dma((2,))],
        )(*traces)

    in_specs = (
        P("gz", None, None, "xy"),
        P("gz", None, None, "xy"),
        P(),
        P("gz", "xy", None, None, None, None),
        P("gz", "xy", None, None, None, None),
        P("gz", "xy", None),
    )
    out_specs = (P("gz", None, None, "xy"), P("gz", None, None, "xy"))
    return jax.shard_map(
        on_device, mesh=mesh, in_specs=in_specs, out_specs=out_specs, check_vma=False
    )
```
